32 devices in a mesh: rows: 8 (over y, x, core), cols: 4 (over z).
Axes of the slice: x: 2, y: 2, z: 4, core: 2. Of those that a mesh axis runs over, the one named last changes fastest.
Arguments:
- field: bfloat16 [32, 512, 512], P(None, 'rows', 'cols'), may hold values from -6 to 6
- cotangent: bfloat16 [32, 512, 512], P(None, 'rows', 'cols'), may hold values from -6 to 6
- weight_real: bfloat16 [32, 32, 8192], P(None, None, ('rows', 'cols')), may hold values from -0.75 to 0.75
- weight_imag: bfloat16 [32, 32, 8192], P(None, None, ('rows', 'cols')), may hold values from -0.75 to 0.75
- kernel: bfloat16 [3, 3, 32, 32], replicated, may hold values from -0.375 to 0.375
Outputs:
- layer_out: bfloat16 [32, 512, 512], P(None, 'rows', 'cols')
- field_grad: bfloat16 [32, 512, 512], P(None, 'rows', 'cols')
- weight_grad_real: float32 [32, 32, 8192], P(None, None, ('rows', 'cols'))
- weight_grad_imag: float32 [32, 32, 8192], P(None, None, ('rows', 'cols'))
- kernel_grad: float32 [3, 3, 32, 32], replicated
The draws below stay inside these ranges and needn't reach their ends.
All inputs are finite; a program needn't handle non-finite values.
Results may differ from the reference program's by a relative error of at most 0.0068.
Values may be sent and summed in bfloat16 or wider, within the bound.
No kernel may reach another device: no remote copies, remote signals or barrier semaphores. Data moves between devices by JAX's collectives and lax.ppermute only.
A program may use at most 128 MiB of HBM per device.

```python
import math
import jax
import jax.numpy as jnp
from jax import lax

C = 32
M = 64
NX = 512
NY = 512


def shard_levels(stream_key, shape, pieces, least, top_value):
    level = 1.0
    for position, blocks in pieces:
        heights = jax.random.uniform(jax.random.fold_in(jax.random.fold_in(stream_key, 6), position), (blocks,), jnp.float32, least / len(pieces), top_value / len(pieces))
        level = level * jnp.repeat(jnp.exp(heights), shape[position] // blocks).reshape((-1,) + (1,) * (len(shape) - 1 - position))
    return level


def noise(key, extent, spread, bound, split=(), kind=jnp.bfloat16):
    drawn = jax.random.normal(key, extent, jnp.float32) * spread
    if len(split) > 0:
        drawn = shard_levels(key, extent, split, -0.22, 0.18) * drawn
    return jnp.clip(drawn, min=-bound, max=bound).astype(kind)


def setup_inputs(seed: int = 0) -> dict:
    arg_keys = jax.random.split(jax.random.key(seed), 6)
    return {
        "field": noise(arg_keys[0], (C, NX, NY), 1.0, 6.0, ((1, 8), (2, 4))),
        "cotangent": noise(arg_keys[1], (C, NX, NY), 1.0, 6.0, ((1, 8), (2, 4))),
        "weight_real": noise(arg_keys[2], (C, C, 2 * M * M), (2 * C) ** -0.5, 0.75, ((2, 32),)),
        "weight_imag": noise(arg_keys[3], (C, C, 2 * M * M), (2 * C) ** -0.5, 0.75, ((2, 32),)),
        "kernel": noise(arg_keys[4], (3, 3, C, C), (9 * C) ** -0.5, 0.375),
    }


highest = lax.Precision.HIGHEST

def tables(count_modes, offset, local, total):
    modes = jnp.arange(count_modes, dtype=jnp.int32)
    cells = offset + jnp.arange(local, dtype=jnp.int32)
    phase = modes[:, None] * cells[None, :] % total
    angle = phase.astype(jnp.float32) * (2.0 * math.pi / total)
    return (jnp.cos(angle), jnp.sin(angle))

def row_tables(count_modes, offset, local, total):
    base = jnp.arange(count_modes, dtype=jnp.int32)
    modes = jnp.concatenate([base, (total - count_modes + base).astype(jnp.int32)])
    cells = offset + jnp.arange(local, dtype=jnp.int32)
    phase = modes[:, None] * cells[None, :] % total
    angle = phase.astype(jnp.float32) * (2.0 * math.pi / total)
    return (jnp.cos(angle), jnp.sin(angle))

def product(form, left, right):
    return jnp.einsum(form, left.astype(jnp.float32), right.astype(jnp.float32), precision=highest)

def smooth(values):
    return jax.nn.gelu(values, approximate=True)

def convolve(inputs, weights):
    return lax.conv_general_dilated(inputs[None], weights, (1, 1), ((1, 1), (1, 1)), precision=highest)[0]

def reference(field, cotangent, weight_real, weight_imag, kernel):
    cos_rows, sin_rows = row_tables(M, 0, NX, NX)
    cos_cols, sin_cols = tables(M, 0, NY, NY)
    scale_rows = 1.0 / math.sqrt(NX)
    scale_cols = 1.0 / math.sqrt(NY)
    scale_cells = 1.0 / math.sqrt(NX * NY)
    cos_cols_half = (cos_cols * scale_cols).astype(jnp.bfloat16)
    sin_cols_half = (-(sin_cols * scale_cols)).astype(jnp.bfloat16)
    half_real = product('cij,bj->cib', field, cos_cols_half)
    half_imag = product('cij,bj->cib', field, sin_cols_half)
    cos_rows_scaled = cos_rows * scale_rows
    sin_rows_scaled = sin_rows * scale_rows
    coef_real = product('ai,cib->cab', cos_rows_scaled, half_real) + product('ai,cib->cab', sin_rows_scaled, half_imag)
    coef_imag = product('ai,cib->cab', cos_rows_scaled, half_imag) - product('ai,cib->cab', sin_rows_scaled, half_real)
    coef_real = coef_real.reshape(C, 2 * M * M)
    coef_imag = coef_imag.reshape(C, 2 * M * M)
    wide_real = weight_real.astype(jnp.float32)
    wide_imag = weight_imag.astype(jnp.float32)
    mixed_real = product('cm,com->om', coef_real, wide_real) - product('cm,com->om', coef_imag, wide_imag)
    mixed_imag = product('cm,com->om', coef_real, wide_imag) + product('cm,com->om', coef_imag, wide_real)
    mixed_real = mixed_real.astype(jnp.bfloat16).reshape(C, 2 * M, M)
    mixed_imag = mixed_imag.astype(jnp.bfloat16).reshape(C, 2 * M, M)
    cos_rows_half = cos_rows.astype(jnp.bfloat16)
    sin_rows_half = sin_rows.astype(jnp.bfloat16)
    back_real = product('ai,oab->oib', cos_rows_half, mixed_real) - product('ai,oab->oib', sin_rows_half, mixed_imag)
    back_imag = product('ai,oab->oib', cos_rows_half, mixed_imag) + product('ai,oab->oib', sin_rows_half, mixed_real)
    spectral = (product('oib,bj->oij', back_real, cos_cols) - product('oib,bj->oij', back_imag, sin_cols)) / M
    kernel_wide = kernel.astype(jnp.float32)
    forward_weights = jnp.transpose(kernel_wide, (3, 2, 0, 1))
    preact = spectral + convolve(field.astype(jnp.float32), forward_weights)
    activated, pullback = jax.vjp(smooth, preact)
    grad_pre = pullback(cotangent.astype(jnp.float32))[0].astype(jnp.bfloat16)
    cos_cols_plain = cos_cols.astype(jnp.bfloat16)
    sin_cols_plain = sin_cols.astype(jnp.bfloat16)
    grad_back_real = product('oij,bj->oib', grad_pre, cos_cols_plain) / M
    grad_back_imag = -product('oij,bj->oib', grad_pre, sin_cols_plain) / M
    grad_real = product('ai,oib->oab', cos_rows, grad_back_real) + product('ai,oib->oab', sin_rows, grad_back_imag)
    grad_imag = product('ai,oib->oab', cos_rows, grad_back_imag) - product('ai,oib->oab', sin_rows, grad_back_real)
    mode_real = grad_real.reshape(C, 2 * M * M)
    mode_imag = grad_imag.reshape(C, 2 * M * M)
    weight_scale = M * scale_cells
    out_real = (coef_real[:, None, :] * mode_real[None] + coef_imag[:, None, :] * mode_imag[None]) * weight_scale
    out_imag = (coef_real[:, None, :] * mode_imag[None] - coef_imag[:, None, :] * mode_real[None]) * weight_scale
    input_real = product('com,om->cm', wide_real, mode_real) + product('com,om->cm', wide_imag, mode_imag)
    input_imag = product('com,om->cm', wide_real, mode_imag) - product('com,om->cm', wide_imag, mode_real)
    input_real = input_real.astype(jnp.bfloat16).reshape(C, 2 * M, M)
    input_imag = input_imag.astype(jnp.bfloat16).reshape(C, 2 * M, M)
    cos_scaled_half = cos_rows_scaled.astype(jnp.bfloat16)
    sin_scaled_half = sin_rows_scaled.astype(jnp.bfloat16)
    line_real = product('ai,cab->cib', cos_scaled_half, input_real) - product('ai,cab->cib', sin_scaled_half, input_imag)
    line_imag = product('ai,cab->cib', sin_scaled_half, input_real) + product('ai,cab->cib', cos_scaled_half, input_imag)
    spectral_grad = product('cib,bj->cij', line_real, cos_cols * scale_cols) - product('cib,bj->cij', line_imag, sin_cols * scale_cols)
    backward_weights = jnp.transpose(kernel_wide[::-1, ::-1], (2, 3, 0, 1))
    conv_grad = convolve(grad_pre.astype(jnp.float32), backward_weights)
    field_grad = (spectral_grad + conv_grad).astype(jnp.bfloat16)
    padded = jnp.pad(field.astype(jnp.float32), ((0, 0), (1, 1), (1, 1)))
    kernel_terms = []
    for row_step in range(3):
        for col_step in range(3):
            window = padded[:, row_step:row_step + NX, col_step:col_step + NY]
            kernel_terms.append(product('cij,oij->co', window, grad_pre))
    kernel_grad = jnp.stack(kernel_terms).reshape(3, 3, C, C) * scale_cells
    return (activated.astype(jnp.bfloat16), field_grad, out_real, out_imag, kernel_grad)
```

```python
import functools
import math

import jax
import jax.numpy as jnp
import numpy as np
from jax import lax
from jax.experimental import pallas as pl
from jax.experimental.pallas import tpu as pltpu
from jax.sharding import PartitionSpec as P

M = 64
BLOCK = 8
f32 = jnp.float32
bf16 = jnp.bfloat16
BOTH = ("rows", "cols")


def dot(left, right):
    return jnp.dot(left, right, preferred_element_type=f32)


def dot_nt(left, right):
    return lax.dot_general(
        left, right, (((1,), (1,)), ((), ())), preferred_element_type=f32
    )


def call(kernel, out_shape, scratch, flops, moved, *args):
    return pl.pallas_call(
        kernel,
        out_shape=out_shape,
        in_specs=[pl.BlockSpec(memory_space=pltpu.VMEM)] * len(args),
        out_specs=jax.tree.map(lambda _: pl.BlockSpec(memory_space=pltpu.VMEM), out_shape),
        scratch_shapes=scratch,
        compiler_params=pltpu.CompilerParams(vmem_limit_bytes=40 << 20),
        cost_estimate=pl.CostEstimate(flops=flops, bytes_accessed=moved, transcendentals=0),
    )(*args)


def shape(dims, dtype):
    return jax.ShapeDtypeStruct(dims, dtype)


def row_angles(total, places):
    modes = np.concatenate([np.arange(M), total - M + np.arange(M)])
    phase = modes[:, None] * np.arange(total)[None, :] % total
    angle = phase * (2.0 * np.pi / total)
    local = total // places
    cut = lambda t: t.reshape(2 * M, places, local).transpose(1, 0, 2)
    return cut(np.cos(angle)), cut(np.sin(angle))


def col_angles(total, places):
    phase = np.arange(M)[:, None] * np.arange(total)[None, :] % total
    angle = phase * (2.0 * np.pi / total)
    local = total // places
    cut = lambda t: t.reshape(M, places, local).transpose(1, 0, 2)
    return cut(np.cos(angle)), cut(np.sin(angle))


def make_tables(rows_here, cols_here):
    places_rows, places_cols = lax.axis_size("rows"), lax.axis_size("cols")
    total_rows, total_cols = rows_here * places_rows, cols_here * places_cols
    cx, sx = row_angles(total_rows, places_rows)
    cy, sy = col_angles(total_cols, places_cols)
    scale_rows, scale_cols = 1.0 / math.sqrt(total_rows), 1.0 / math.sqrt(total_cols)
    turn = lambda t: t.transpose(0, 2, 1)

    def to_modes(c, s):
        return np.concatenate([turn(c), -turn(s), -turn(s), -turn(c)], axis=2)

    def to_cells(c, s):
        return np.concatenate([c, -s, -s, -c], axis=1)

    def rows_out(c, s):
        return np.concatenate([c, s], axis=2)

    def rows_back(c, s):
        return np.concatenate([turn(c), turn(s)], axis=1)

    row_index, col_index = lax.axis_index("rows"), lax.axis_index("cols")

    def pick(table, index):
        held = jnp.asarray(table.astype(np.float32)).astype(bf16)
        return lax.dynamic_index_in_dim(held, index, 0, keepdims=False)

    return {
        "cols_forward": pick(to_modes(cy * scale_cols, sy * scale_cols), col_index),
        "rows_forward": pick(rows_out(cx * scale_rows, sx * scale_rows), row_index),
        "rows_inverse": pick(rows_back(cx, sx), row_index),
        "cols_inverse": pick(to_cells(cy, sy) / M, col_index),
        "cols_grad": pick(to_modes(cy, sy), col_index),
        "rows_grad": pick(rows_out(cx, sx) / M, row_index),
        "rows_last": pick(rows_back(cx * scale_rows, sx * scale_rows), row_index),
        "cols_last": pick(to_cells(cy * scale_cols, sy * scale_cols), col_index),
    }


def pair_to_modes(cells, cols_table, rows_table):
    height = cells.shape[0] // 2
    width = cols_table.shape[1] // 2
    lines = dot(cells, cols_table).astype(bf16)
    first = jnp.concatenate([lines[:height, :width], lines[:height, width:]], axis=0)
    second = jnp.concatenate([lines[height:, :width], lines[height:, width:]], axis=0)
    return dot(rows_table, jnp.concatenate([first, second], axis=1))


def pair_to_cells(first, second, rows_table, cols_table):
    width = first.shape[1]
    lines = dot(rows_table, jnp.concatenate([first, second], axis=1)).astype(bf16)
    height = lines.shape[0] // 2
    top = jnp.concatenate([lines[:height, :width], lines[height:, :width]], axis=1)
    low = jnp.concatenate([lines[:height, width:], lines[height:, width:]], axis=1)
    return dot(jnp.concatenate([top, low], axis=0), cols_table)


def forward_kernel(field_ref, cols_ref, rows_ref, modes_ref, turned_ref, modes_s, turned_s):
    channels, height, _ = field_ref.shape
    width = modes_ref.shape[1]
    cols_table, rows_table = cols_ref[...], rows_ref[...]
    for c in range(0, channels, 2):
        cells = jnp.concatenate([field_ref[c], field_ref[c + 1]], axis=0)
        modes = pair_to_modes(cells, cols_table, rows_table)
        wide = cells.astype(f32)
        for k in range(2):
            modes_s[pl.ds(c + k, 2 * M, stride=channels), :] = modes[:, k * width : (k + 1) * width]
            turned_s[pl.ds(c + k, height, stride=channels), :] = wide[k * height : (k + 1) * height]
    modes_ref[...] = modes_s[...].astype(bf16)
    turned_ref[...] = turned_s[...].astype(bf16)


def middle_kernel(
    modes_ref, conv_ref, cotangent_ref, rows_in_ref, cols_in_ref, cols_ref, rows_ref,
    out_ref, turned_ref, grads_ref, modes_s, grads_s, turned_s,
):
    channels, height, _ = cotangent_ref.shape
    width = modes_ref.shape[1]
    modes_s[...] = modes_ref[...].astype(f32)
    root = math.sqrt(2.0 / math.pi)
    for c in range(0, channels, 2):
        first = modes_s[pl.ds(c, 2 * M, stride=channels), :].astype(bf16)
        second = modes_s[pl.ds(c + 1, 2 * M, stride=channels), :].astype(bf16)
        cells = pair_to_cells(first, second, rows_in_ref[...], cols_in_ref[...])
        kept = []
        for k in range(2):
            pre = cells[k * height : (k + 1) * height]
            pre = pre + conv_ref[pl.ds(c + k, height, stride=channels), :]
            square = pre * pre
            turn = jnp.tanh(root * (pre + 0.044715 * (square * pre)))
            half = 0.5 * (1.0 + turn)
            out_ref[c + k] = (pre * half).astype(bf16)
            slope = half + 0.5 * pre * (1.0 - turn * turn) * (root * (1.0 + 0.134145 * square))
            grad = (cotangent_ref[c + k].astype(f32) * slope).astype(bf16)
            turned_s[pl.ds(c + k, height, stride=channels), :] = grad.astype(f32)
            kept.append(grad)
        grads = pair_to_modes(jnp.concatenate(kept, axis=0), cols_ref[...], rows_ref[...])
        for k in range(2):
            grads_s[pl.ds(c + k, 2 * M, stride=channels), :] = grads[:, k * width : (k + 1) * width]
    grads_ref[...] = grads_s[...].astype(bf16)
    turned_ref[...] = turned_s[...].astype(bf16)


def last_kernel(modes_ref, conv_ref, rows_in_ref, cols_in_ref, out_ref, modes_s):
    channels, height, _ = out_ref.shape
    modes_s[...] = modes_ref[...].astype(f32)
    for c in range(0, channels, 2):
        first = modes_s[pl.ds(c, 2 * M, stride=channels), :].astype(bf16)
        second = modes_s[pl.ds(c + 1, 2 * M, stride=channels), :].astype(bf16)
        cells = pair_to_cells(first, second, rows_in_ref[...], cols_in_ref[...])
        for k in range(2):
            total = cells[k * height : (k + 1) * height]
            total = total + conv_ref[pl.ds(c + k, height, stride=channels), :]
            out_ref[c + k] = total.astype(bf16)


def band(weights):
    outs = weights.shape[3]
    flat = jnp.transpose(weights, (3, 0, 1, 2)).reshape(outs, -1)
    step = flat.shape[1] // 3
    rows = [
        jnp.pad(flat, ((0, 0), (step * k, step * (BLOCK - 1 - k)))) for k in range(BLOCK)
    ]
    return jnp.concatenate(rows, axis=0)


def stencil_kernel(cells_ref, band_ref, out_ref):
    height, lines, width = cells_ref.shape
    rows = band_ref.shape[0]
    matrix = band_ref[...]
    for b in range(0, (height - 2) // BLOCK, 2):
        pair = [
            cells_ref[BLOCK * k : BLOCK * k + BLOCK + 2].reshape((BLOCK + 2) * lines, width)
            for k in (b, b + 1)
        ]
        both = dot(matrix, jnp.concatenate(pair, axis=1))
        for k in range(2):
            out_ref[rows * (b + k) : rows * (b + k + 1), :] = both[:, k * width : (k + 1) * width]


def stencil(cells, matrix, channels):
    height, lines, width = cells.shape
    return call(
        stencil_kernel,
        shape(((height - 2) * channels, width), f32),
        [],
        2 * matrix.size * height * width // BLOCK,
        cells.size * 2 + matrix.size * 2 + height * channels * width * 4,
        cells, matrix,
    )


def kernel_grad_kernel(cells_ref, grad_ref, out_ref):
    height, lines, width = cells_ref.shape
    channels = grad_ref.shape[1]
    taken = BLOCK * channels
    total = jnp.zeros(((BLOCK + 2) * lines, taken), f32)
    for b in range(0, (height - 2) // BLOCK, 2):
        cells = [
            cells_ref[BLOCK * k : BLOCK * k + BLOCK + 2].reshape((BLOCK + 2) * lines, width)
            for k in (b, b + 1)
        ]
        grads = [
            grad_ref[BLOCK * k : BLOCK * (k + 1)].reshape(taken, width) for k in (b, b + 1)
        ]
        total = total + dot_nt(jnp.concatenate(cells, axis=1), jnp.concatenate(grads, axis=1))
    place = lax.broadcasted_iota(jnp.int32, (3 * lines, taken), 1) // channels
    folded = jnp.zeros((3 * lines, taken), f32)
    for k in range(BLOCK):
        folded = folded + jnp.where(place == k, total[lines * k : lines * (k + 3)], 0.0)
    size = taken
    while size > 128:
        size //= 2
        folded = folded[:, :size] + folded[:, size : 2 * size]
    step = size // 2
    while step >= channels:
        folded = folded + pltpu.roll(folded, step, 1)
        step //= 2
    out_ref[...] = folded


def kernel_grad_here(cells, grad):
    height, lines, width = cells.shape
    return call(
        kernel_grad_kernel,
        shape((3 * lines, 128), f32),
        [],
        2 * cells.size * BLOCK * grad.shape[1],
        cells.size * 2 + grad.size * 2,
        cells, grad,
    )


def widened(turned):
    count_rows, count_cols = lax.axis_size("rows"), lax.axis_size("cols")
    up = [(i, i + 1) for i in range(count_rows - 1)]
    down = [(i + 1, i) for i in range(count_rows - 1)]
    before = lax.ppermute(turned[-1:], "rows", up)
    after = lax.ppermute(turned[:1], "rows", down)
    tall = jnp.concatenate([before, turned, after], axis=0)
    right = [(i, i + 1) for i in range(count_cols - 1)]
    left = [(i + 1, i) for i in range(count_cols - 1)]
    first = lax.ppermute(tall[:, :, -1], "cols", right)[:, :, None]
    final = lax.ppermute(tall[:, :, 0], "cols", left)[:, :, None]
    return jnp.concatenate(
        [
            jnp.concatenate([first, tall[:, :, :-1]], axis=2),
            tall,
            jnp.concatenate([tall[:, :, 1:], final], axis=2),
        ],
        axis=1,
    )


def total_sum(values):
    for axis in ("rows", "cols"):
        count, step = lax.axis_size(axis), 1
        while step < count:
            swap = [(i, i ^ step) for i in range(count)]
            values = values + lax.ppermute(values, axis, swap)
            step *= 2
    return values


def halves(total):
    low = lax.broadcasted_iota(jnp.int32, total[0].shape, 1) < M
    real, imag = [], []
    for t in range(0, len(total), 2):
        one, two = total[t], total[t + 1]
        real.append(jnp.where(low, one, pltpu.roll(two, M, 1)))
        imag.append(jnp.where(low, pltpu.roll(one, M, 1), two))
    return jnp.concatenate(real, axis=1), jnp.concatenate(imag, axis=1)


def unhalved(real, imag):
    low = lax.broadcasted_iota(jnp.int32, (real.shape[0], 2 * M), 1) < M
    rows = []
    for t in range(0, real.shape[1], 2 * M):
        re, im = real[:, t : t + 2 * M], imag[:, t : t + 2 * M]
        rows.append(jnp.where(low, re, pltpu.roll(im, M, 1)))
        rows.append(jnp.where(low, pltpu.roll(re, M, 1), im))
    return rows


def gathered_rows(parts_ref, channels):
    devices, lines, _ = parts_ref.shape
    total = parts_ref[0].astype(f32)
    for d in range(1, devices):
        total = total + parts_ref[d].astype(f32)
    return [total[k : k + channels] for k in range(0, lines, channels)]


def send_all(rows, out_ref, channels):
    for k, row in enumerate(rows):
        value = row.astype(bf16)
        for d in range(out_ref.shape[0]):
            out_ref[d, k * channels : (k + 1) * channels, :] = value


def mix_kernel(parts_ref, real_ref, imag_ref, out_ref, coef_real_ref, coef_imag_ref):
    channels = real_ref.shape[0]
    real, imag = halves(gathered_rows(parts_ref, channels))
    coef_real_ref[...] = real
    coef_imag_ref[...] = imag
    mixed_real = jnp.zeros(real_ref.shape[1:], f32)
    mixed_imag = jnp.zeros(real_ref.shape[1:], f32)
    for c in range(channels):
        wr, wi = real_ref[c].astype(f32), imag_ref[c].astype(f32)
        re, im = real[c : c + 1], imag[c : c + 1]
        mixed_real = mixed_real + (re * wr - im * wi)
        mixed_imag = mixed_imag + (re * wi + im * wr)
    send_all(unhalved(mixed_real, mixed_imag), out_ref, channels)


def unmix_kernel(parts_ref, real_ref, imag_ref, out_ref, mode_real_ref, mode_imag_ref, re_s, im_s):
    channels = real_ref.shape[0]
    real, imag = halves(gathered_rows(parts_ref, channels))
    mode_real_ref[...] = real
    mode_imag_ref[...] = imag
    for c in range(channels):
        wr, wi = real_ref[c].astype(f32), imag_ref[c].astype(f32)
        re_s[c : c + 1, :] = jnp.sum(wr * real + wi * imag, axis=0, keepdims=True)
        im_s[c : c + 1, :] = jnp.sum(wr * imag - wi * real, axis=0, keepdims=True)
    send_all(unhalved(re_s[...], im_s[...]), out_ref, channels)


def owner_stage(kernel, parts, real, imag, extra):
    channels, _, modes = real.shape
    return call(
        kernel,
        (shape(parts.shape, bf16), shape((channels, modes), f32), shape((channels, modes), f32)),
        [pltpu.VMEM((channels, modes), f32)] * extra,
        8 * real.size,
        parts.size * 4 + real.size * 4,
        parts, real, imag,
    )


def exact(form, left, right):
    return jnp.einsum(form, left, right, precision=lax.Precision.HIGHEST, preferred_element_type=f32)


def at_owner(partial, weight_real, weight_imag, forward):
    channels, _, modes = weight_real.shape
    devices = 2 * M * M // modes
    swap = lambda x: lax.all_to_all(x, BOTH, 0, 0, tiled=True)
    if modes % (2 * M) == 0 and M == 64:
        parts = swap(partial.reshape(devices, modes // M * channels, 2 * M))
        kernel = mix_kernel if forward else unmix_kernel
        sent, real, imag = owner_stage(kernel, parts, weight_real, weight_imag, 0 if forward else 2)
        return swap(sent).reshape(2 * M * channels, 2 * M), real, imag
    pieces = M // modes
    parts = partial.reshape(2 * M, channels, 2, pieces, modes).transpose(0, 3, 1, 2, 4)
    parts = swap(parts.reshape(devices, channels, 2, modes))
    total = jnp.sum(parts.astype(f32), axis=0)
    real, imag = total[:, 0], total[:, 1]
    wr, wi = weight_real.astype(f32), weight_imag.astype(f32)
    if forward:
        re = exact("cm,com->om", real, wr) - exact("cm,com->om", imag, wi)
        im = exact("cm,com->om", real, wi) + exact("cm,com->om", imag, wr)
    else:
        re = exact("com,om->cm", wr, real) + exact("com,om->cm", wi, imag)
        im = exact("com,om->cm", wr, imag) - exact("com,om->cm", wi, real)
    sent = jnp.stack([re, im], axis=1).astype(bf16)
    sent = swap(jnp.broadcast_to(sent, (devices,) + sent.shape))
    spread = sent.reshape(2 * M, pieces, channels, 2, modes).transpose(0, 2, 3, 1, 4)
    return spread.reshape(2 * M * channels, 2 * M), real, imag


def body(field, cotangent, weight_real, weight_imag, kernel):
    channels, rows_here, cols_here = field.shape
    total_rows = rows_here * lax.axis_size("rows")
    total_cols = cols_here * lax.axis_size("cols")
    scale_cells = 1.0 / math.sqrt(total_rows * total_cols)
    table = make_tables(rows_here, cols_here)
    cells = field.size
    lines = (2 * M * channels, 2 * M)
    turned_lines = (rows_here * channels, cols_here)
    transform = 2 * cells * 4 * M + 2 * lines[0] * lines[1] * 2 * rows_here

    partial, turned = call(
        forward_kernel,
        (shape(lines, bf16), shape(turned_lines, bf16)),
        [pltpu.VMEM(lines, f32), pltpu.VMEM(turned_lines, f32)],
        transform, cells * 4 + lines[0] * lines[1] * 2,
        field, table["cols_forward"], table["rows_forward"],
    )
    spectrum, coef_real, coef_imag = at_owner(partial, weight_real, weight_imag, True)

    wide_field = widened(turned.reshape(rows_here, channels, cols_here))
    conv = stencil(wide_field, band(kernel), channels)

    activated, grad_turned, partial_grad = call(
        middle_kernel,
        (shape(field.shape, bf16), shape(turned_lines, bf16), shape(lines, bf16)),
        [pltpu.VMEM(lines, f32), pltpu.VMEM(lines, f32), pltpu.VMEM(turned_lines, f32)],
        2 * transform, cells * 10 + lines[0] * lines[1] * 4,
        spectrum, conv, cotangent, table["rows_inverse"], table["cols_inverse"],
        table["cols_grad"], table["rows_grad"],
    )
    spectrum_grad, mode_real, mode_imag = at_owner(partial_grad, weight_real, weight_imag, False)

    grad_turned = grad_turned.reshape(rows_here, channels, cols_here)
    wide_grad = widened(grad_turned)
    backward = jnp.transpose(kernel[::-1, ::-1], (0, 1, 3, 2))
    conv_grad = stencil(wide_grad, band(backward), channels)
    local = kernel_grad_here(wide_field, grad_turned)[:, :channels]
    kernel_grad = total_sum(local).reshape(3, 3, channels, channels) * scale_cells

    weight_scale = M * scale_cells
    out_real = (
        coef_real[:, None, :] * mode_real[None] + coef_imag[:, None, :] * mode_imag[None]
    ) * weight_scale
    out_imag = (
        coef_real[:, None, :] * mode_imag[None] - coef_imag[:, None, :] * mode_real[None]
    ) * weight_scale

    field_grad = call(
        last_kernel,
        shape(field.shape, bf16),
        [pltpu.VMEM(lines, f32)],
        transform, cells * 6 + lines[0] * lines[1] * 2,
        spectrum_grad, conv_grad, table["rows_last"], table["cols_last"],
    )
    return activated, field_grad, out_real, out_imag, kernel_grad


def solution(mesh):
    placed = (
        P(None, "rows", "cols"),
        P(None, "rows", "cols"),
        P(None, None, ("rows", "cols")),
        P(None, None, ("rows", "cols")),
        P(),
    )
    return jax.shard_map(
        body, mesh=mesh, in_specs=placed, out_specs=placed, check_vma=False
    )
```

```python
import functools
import math

import jax
import jax.numpy as jnp
import numpy as np
from jax import lax
from jax.experimental import pallas as pl
from jax.experimental.pallas import tpu as pltpu
from jax.sharding import PartitionSpec as P

M = 64
BLOCK = 8
QUAD = 8
f32 = jnp.float32
bf16 = jnp.bfloat16
ROWS = ("chips", "core")
BOTH = ("chips", "core", "cols")


def dot(left, right):
    return jnp.dot(left, right, preferred_element_type=f32)


def dot_tn(left, right):
    return lax.dot_general(
        left, right, (((0,), (0,)), ((), ())), preferred_element_type=f32
    )


def dot_nt(left, right):
    return lax.dot_general(
        left, right, (((1,), (1,)), ((), ())), preferred_element_type=f32
    )


def call(kernel, out_shape, scratch, flops, moved, *args, far=0):
    near = [pl.BlockSpec(memory_space=pltpu.VMEM)] * (len(args) - far)
    return pl.pallas_call(
        kernel,
        out_shape=out_shape,
        in_specs=[pl.BlockSpec(memory_space=pltpu.HBM)] * far + near,
        out_specs=jax.tree.map(lambda _: pl.BlockSpec(memory_space=pltpu.VMEM), out_shape),
        scratch_shapes=scratch,
        compiler_params=pltpu.CompilerParams(vmem_limit_bytes=20 << 20),
        cost_estimate=pl.CostEstimate(flops=flops, bytes_accessed=moved, transcendentals=0),
    )(*args)


def shape(dims, dtype):
    return jax.ShapeDtypeStruct(dims, dtype)


def row_table(total, places):
    modes = np.concatenate([np.arange(M), total - M + np.arange(M)])
    phase = modes[:, None] * np.arange(total)[None, :] % total
    angle = (phase * (2.0 * np.pi / total)).reshape(2 * M, places, total // places)
    c, s = np.cos(angle).transpose(1, 0, 2), np.sin(angle).transpose(1, 0, 2)
    table = np.stack([np.concatenate([c, s], 2), np.concatenate([-s, c], 2)], axis=2)
    return table.reshape(places, 4 * M, 2 * (total // places)).astype(np.float32)


def col_table(total, places):
    phase = np.arange(total)[:, None] * np.arange(M)[None, :] % total
    angle = (phase * (2.0 * np.pi / total)).reshape(places, total // places, M)
    c, s = np.cos(angle), -np.sin(angle)
    none = np.zeros_like(c)
    even = np.concatenate([c, none, s, none], axis=2)
    odd = np.concatenate([none, c, none, s], axis=2)
    return np.concatenate([even, odd], axis=1).astype(np.float32)


def split(table):
    high = table.astype(bf16)
    return high, (table - high.astype(f32)).astype(bf16)


class Plan:
    def __init__(self, channels):
        self.chips, self.cores, self.cols = (lax.axis_size(a) for a in BOTH)
        self.devices = self.chips * self.cores * self.cols
        self.block = 4 * channels
        self.blocks = M // 2
        self.staged = M == 64 and self.devices == self.blocks

    def shapes(self, dtype):
        if not self.staged:
            return (shape((self.blocks * self.block, 2 * M), dtype),)
        return (shape((self.cols * self.block, 2 * M), dtype),) * (self.cores * self.chips)

    def places(self):
        if not self.staged:
            return [(0, k * self.block) for k in range(self.blocks)]
        return [
            (k, q * self.block) for k in range(self.cores * self.chips) for q in range(self.cols)
        ]

    def rows(self, table_ref):
        if not self.staged:
            return table_ref[...]
        chip, core, col = (lax.axis_index(a) for a in BOTH)
        found = []
        for k in range(self.cores):
            for h in range(self.chips):
                for q in range(self.cols):
                    owner = ((chip ^ h) * self.cores + (core ^ k)) * self.cols + (col ^ q)
                    found.append(table_ref[pl.ds(pl.multiple_of(owner * 8, 8), 8), :])
        return jnp.concatenate(found, axis=0)


def forward_rows(rows):
    return jnp.concatenate(split(rows), axis=1)


def quad_to_modes(plan, cells, cols_table, rows_table, pieces, at):
    height, _ = cells[0].shape
    pairs = [jnp.concatenate(cells[k : k + 2], axis=1) for k in range(0, len(cells), 2)]
    lines = dot(jnp.concatenate(pairs, axis=0), cols_table).astype(bf16)
    for t in range(0, len(pairs), 2):
        sides = []
        for p in (t, t + 1):
            part = lines[p * height : (p + 1) * height]
            sides.append(jnp.concatenate([part[:, : 2 * M], part[:, 2 * M :]], axis=0))
        right = jnp.concatenate(sides, axis=1)
        modes = dot(rows_table, jnp.concatenate([right, right], axis=0))
        for k, (piece, row) in enumerate(plan.places()):
            block = modes[8 * k : 8 * k + 8]
            block = jnp.concatenate([block[:, : 2 * M], block[:, 2 * M :]], axis=0)
            start = row + at + 8 * t
            pieces[piece][start : start + 16, :] = block.astype(bf16)


def quad_to_cells(plan, pieces, at, rows_table, cols_high, cols_low, count):
    stacked = []
    for t in range(0, count // 2, 2):
        first, second = [], []
        for piece, row in plan.places():
            block = pieces[piece][row + at + 8 * t : row + at + 8 * t + 16, :].astype(f32)
            first.append(block[:8])
            second.append(block[8:])
        modes = jnp.concatenate(
            [jnp.concatenate(first, axis=0), jnp.concatenate(second, axis=0)], axis=1
        )
        lines = dot(rows_table, modes.astype(bf16)).astype(bf16)
        height = lines.shape[0] // 2
        for p in (0, 1):
            lanes = slice(2 * M * p, 2 * M * (p + 1))
            stacked.append(jnp.concatenate([lines[:height, lanes], lines[height:, lanes]], axis=1))
    stacked = jnp.concatenate(stacked, axis=0)
    cells = dot_nt(stacked, cols_high) + dot_nt(stacked, cols_low)
    width = cells.shape[1] // 2
    return [
        cells[(k // 2) * height : (k // 2 + 1) * height, (k % 2) * width : (k % 2 + 1) * width]
        for k in range(count)
    ]


def forward_kernel(plan, scale_rows, scale_cols, field_ref, cols_all, rows_all, *refs):
    pieces, (field_s, cols_s, rows_s, sems) = refs[:-4], refs[-4:]
    channels = field_ref.shape[0]
    steps = channels // QUAD
    copies = [
        pltpu.make_async_copy(rows_all.at[lax.axis_index(ROWS)], rows_s, sems.at[0]),
        pltpu.make_async_copy(cols_all.at[lax.axis_index("cols")], cols_s, sems.at[1]),
    ]
    for k in range(steps):
        part = pl.ds(k * QUAD, QUAD)
        copies.append(pltpu.make_async_copy(field_ref.at[part], field_s.at[part], sems.at[2 + k]))
    for copy in copies:
        copy.start()
    copies[0].wait()
    rows_table = forward_rows(plan.rows(rows_s) * scale_rows)
    copies[1].wait()
    cols_table = (cols_s[...] * scale_cols).astype(bf16)
    for k in range(steps):
        copies[2 + k].wait()
        cells = [field_s[k * QUAD + c] for c in range(QUAD)]
        quad_to_modes(plan, cells, cols_table, rows_table, pieces, k * QUAD * 4)


def middle_kernel(plan, count, *refs):
    modes, refs = refs[:count], refs[count:]
    conv_ref, cotangent_ref, rows_ref, cols_ref, out_ref, grad_ref = refs[:6]
    pieces = refs[6:]
    channels = cotangent_ref.shape[0]
    rows = plan.rows(rows_ref)
    rows_in = (rows.T.astype(bf16).astype(f32) / M).astype(bf16)
    rows_out = forward_rows(rows / M)
    cols_high, cols_low = split(cols_ref[...])
    root = math.sqrt(2.0 / math.pi)
    for at in range(0, channels, QUAD):
        cells = quad_to_cells(plan, modes, at * 4, rows_in, cols_high, cols_low, QUAD)
        kept = []
        for k in range(QUAD):
            pre = cells[k] + conv_ref[at + k]
            square = pre * pre
            turn = jnp.tanh(root * (pre + 0.044715 * (square * pre)))
            half = 0.5 * (1.0 + turn)
            out_ref[at + k] = (pre * half).astype(bf16)
            slope = half + 0.5 * pre * (1.0 - turn * turn) * (root * (1.0 + 0.134145 * square))
            grad = (cotangent_ref[at + k].astype(f32) * slope).astype(bf16)
            grad_ref[at + k] = grad
            kept.append(grad)
        quad_to_modes(plan, kept, cols_high, rows_out, pieces, at * 4)


def last_kernel(plan, count, scale_rows, scale_cols, *refs):
    modes = refs[:count]
    conv_ref, rows_ref, cols_ref, out_ref = refs[count:]
    channels = out_ref.shape[0]
    rows_in = (plan.rows(rows_ref) * scale_rows).T.astype(bf16)
    cols_high, cols_low = split(cols_ref[...] * scale_cols)
    for at in range(0, channels, QUAD):
        cells = quad_to_cells(plan, modes, at * 4, rows_in, cols_high, cols_low, QUAD)
        for k in range(QUAD):
            out_ref[at + k] = (cells[k] + conv_ref[at + k]).astype(bf16)


def turn_kernel(cells_ref, turned_ref, edges_ref, turned_s):
    channels, height, width = cells_ref.shape
    for c in range(channels):
        turned_s[pl.ds(c, height, stride=channels), :] = cells_ref[c].astype(f32)
    turned = turned_s[...].astype(bf16)
    turned_ref[...] = turned
    row = lax.broadcasted_iota(jnp.int32, (16, width), 0)
    col = lax.broadcasted_iota(jnp.int32, (16, width), 1)
    chosen = ((row == 0) & (col == 0)) | ((row == 1) & (col == width - 1))
    edges_ref[...] = dot_nt(chosen.astype(f32).astype(bf16), turned).astype(bf16)


def turn(cells):
    channels, height, width = cells.shape
    lines = (height * channels, width)
    return call(
        turn_kernel,
        (shape(lines, bf16), shape((16, lines[0]), bf16)),
        [pltpu.VMEM(lines, f32)],
        2 * cells.size * 16, cells.size * 4,
        cells,
    )


def band(weights):
    outs = weights.shape[3]
    flat = jnp.transpose(weights, (3, 0, 1, 2)).reshape(outs, -1)
    step = flat.shape[1] // 3
    rows = [
        jnp.pad(flat, ((0, 0), (step * k, step * (BLOCK - 1 - k)))) for k in range(BLOCK)
    ]
    return jnp.concatenate(rows, axis=0)


def stencil_kernel(turned_ref, left_ref, right_ref, top_ref, low_ref, band_ref, out_ref, wide_ref):
    lines, width = turned_ref.shape
    channels = wide_ref.shape[1] // 3
    row = lax.broadcasted_iota(jnp.int32, (2, width), 0)
    col = lax.broadcasted_iota(jnp.int32, (2, width), 1)
    chosen = ((row == 0) & (col == 0)) | ((row == 1) & (col == width - 1))
    chosen = chosen.astype(f32).astype(bf16)
    where = lax.broadcasted_iota(jnp.int32, (channels, width), 1)

    def widen(at, cells, sides):
        count = cells.shape[0] // channels
        halo = dot_tn(sides, chosen)
        wide = cells.astype(f32)
        before, after = pltpu.roll(wide, 1, 1), pltpu.roll(wide, width - 1, 1)
        for k in range(count):
            part = slice(k * channels, (k + 1) * channels)
            wide_ref[at + k, :channels] = jnp.where(where == 0, halo[part], before[part]).astype(bf16)
            wide_ref[at + k, channels : 2 * channels] = cells[part]
            wide_ref[at + k, 2 * channels :] = jnp.where(
                where == width - 1, halo[part], after[part]
            ).astype(bf16)

    widen(0, top_ref[:channels], top_ref[channels : channels + 2, :channels])
    height = lines // channels
    widen(height + 1, low_ref[:channels], low_ref[channels : channels + 2, :channels])
    step = BLOCK * channels
    for b in range(0, lines, step):
        sides = jnp.concatenate([left_ref[:, b : b + step], right_ref[:, b : b + step]], axis=0)
        widen(b // channels + 1, turned_ref[b : b + step], sides)
    matrix = band_ref[...]
    for b in range(0, height // BLOCK, 2):
        pair = [
            wide_ref[BLOCK * k : BLOCK * k + BLOCK + 2].reshape((BLOCK + 2) * 3 * channels, width)
            for k in (b, b + 1)
        ]
        both = dot(matrix, jnp.concatenate(pair, axis=1))
        for k in range(2):
            for i in range(BLOCK):
                line = both[i * channels : (i + 1) * channels, k * width : (k + 1) * width]
                out_ref[pl.ds(BLOCK * (b + k) + i, channels, stride=height), :] = line


def shifted(value, axis, up):
    count = lax.axis_size(axis)
    pairs = [(i, i + 1) if up else (i + 1, i) for i in range(count - 1)]
    return lax.ppermute(value, axis, pairs)


def stencil(turned, edges, matrix, channels):
    lines, width = turned.shape
    height = lines // channels
    left = shifted(edges[1:2], "cols", True)
    right = shifted(edges[0:1], "cols", False)

    def with_sides(cells, at):
        sides = jnp.concatenate([left[:, at : at + channels], right[:, at : at + channels]], axis=0)
        return jnp.concatenate([cells, jnp.pad(sides, ((0, 0), (0, width - channels)))], axis=0)

    top = shifted(with_sides(turned[lines - channels :], lines - channels), ROWS, True)
    low = shifted(with_sides(turned[:channels], 0), ROWS, False)
    conv, wide = call(
        stencil_kernel,
        (shape((lines, width), f32), shape((height + 2, 3 * channels, width), bf16)),
        [],
        2 * matrix.size * height * width // BLOCK,
        lines * width * 12 + matrix.size * 2,
        turned, left, right, top, low, matrix,
    )
    return conv.reshape(channels, height, width), wide


def kernel_grad_kernel(cells_ref, grad_ref, out_ref):
    height, lines, width = cells_ref.shape
    taken = grad_ref.shape[0] * BLOCK // (height - 2)
    channels = taken // BLOCK
    total = jnp.zeros(((BLOCK + 2) * lines, taken), f32)
    for b in range(0, (height - 2) // BLOCK, 2):
        cells = [
            cells_ref[BLOCK * k : BLOCK * k + BLOCK + 2].reshape((BLOCK + 2) * lines, width)
            for k in (b, b + 1)
        ]
        grads = [grad_ref[taken * k : taken * (k + 1)] for k in (b, b + 1)]
        total = total + dot_nt(jnp.concatenate(cells, axis=1), jnp.concatenate(grads, axis=1))
    place = lax.broadcasted_iota(jnp.int32, (3 * lines, taken), 1) // channels
    folded = jnp.zeros((3 * lines, taken), f32)
    for k in range(BLOCK):
        folded = folded + jnp.where(place == k, total[lines * k : lines * (k + 3)], 0.0)
    size = taken
    while size > 128:
        size //= 2
        folded = folded[:, :size] + folded[:, size : 2 * size]
    step = size // 2
    while step >= channels:
        folded = folded + pltpu.roll(folded, step, 1)
        step //= 2
    groups = size // channels
    rows = 3 * lines // groups
    place = lax.broadcasted_iota(jnp.int32, (rows, size), 1) // channels
    packed = jnp.zeros((rows, size), f32)
    for k in range(groups):
        packed = packed + jnp.where(place == k, folded[rows * k : rows * (k + 1)], 0.0)
    out_ref[...] = packed.astype(bf16)


def kernel_grad_here(cells, grad, channels):
    _, lines, _ = cells.shape
    return call(
        kernel_grad_kernel,
        shape((3 * lines * channels // 128, 128), bf16),
        [],
        2 * cells.size * BLOCK * channels,
        cells.size * 2 + grad.size * 2,
        cells, grad,
    )


def swapped(value, axis, step):
    count = lax.axis_size(axis)
    return lax.ppermute(value, axis, [(i, i ^ step) for i in range(count)])


def tree_sum(values):
    values = [v.astype(f32) for v in values]
    while len(values) > 1:
        values = [values[k] + values[k + 1] for k in range(0, len(values), 2)]
    return values[0]


def reduce_pieces(plan, pieces):
    kept, sent = pieces[: plan.chips], pieces[plan.chips :]
    chips = []
    for h in reversed(range(plan.chips)):
        total = kept[h].astype(f32) + swapped(sent[h], "core", 1).astype(f32)
        chips.append(swapped(total.astype(bf16), "chips", h) if h else total)
    total = tree_sum(chips)
    parts = []
    for q in reversed(range(plan.cols)):
        part = total[q * plan.block : (q + 1) * plan.block].astype(bf16)
        parts.append(swapped(part, "cols", q) if q else part)
    return parts


def spread_block(plan, block, extra=None):
    def widen(value, axis, count):
        rows = value.shape[0]
        whole = value if extra is None else jnp.concatenate([value, summed.astype(bf16)], axis=0)
        got = {q: swapped(whole, axis, q) for q in reversed(range(1, count))}
        got[0] = whole
        found = [got[q] for q in range(count)]
        total = None if extra is None else tree_sum([v[rows:] for v in found])
        return [v[:rows] for v in found], total

    summed = extra
    found, summed = widen(block, "cols", plan.cols)
    here = jnp.concatenate(found, axis=0)
    pieces, summed = widen(here, "chips", plan.chips)
    pieces = pieces + [swapped(v, "core", 1) for v in pieces]
    if extra is not None:
        half = summed.astype(bf16)
        summed = tree_sum([half, swapped(half, "core", 1)])
    return pieces, summed


def to_lines(parts, total_s, re_s, im_s):
    total = parts[0][...].astype(f32)
    for part in parts[1:]:
        total = total + part[...].astype(f32)
    total_s[...] = total
    pairs = total.shape[0] // 8
    low = lax.broadcasted_iota(jnp.int32, (pairs, 2 * M), 1) < M
    for side, held in enumerate((re_s, im_s)):
        for t in range(2):
            one = total_s[pl.ds(4 * t + side, pairs, stride=8), :]
            two = total_s[pl.ds(4 * t + 2 + side, pairs, stride=8), :]
            even = jnp.where(low, one, pltpu.roll(two, M, 1))
            odd = jnp.where(low, pltpu.roll(one, M, 1), two)
            held[t, pl.ds(0, pairs, stride=2), :] = even
            held[t, pl.ds(1, pairs, stride=2), :] = odd
    return tuple(jnp.concatenate([held[0], held[1]], axis=1) for held in (re_s, im_s))


def from_lines(real, imag, total_s, re_s, out_ref):
    pairs = real.shape[0] // 2
    low = lax.broadcasted_iota(jnp.int32, (pairs, 2 * M), 1) < M
    for side, value in enumerate((real, imag)):
        for t in range(2):
            re_s[t] = value[:, 2 * M * t : 2 * M * (t + 1)]
            even = re_s[t, pl.ds(0, pairs, stride=2), :]
            odd = re_s[t, pl.ds(1, pairs, stride=2), :]
            one = jnp.where(low, even, pltpu.roll(odd, M, 1))
            two = jnp.where(low, pltpu.roll(even, M, 1), odd)
            total_s[pl.ds(4 * t + side, pairs, stride=8), :] = one
            total_s[pl.ds(4 * t + 2 + side, pairs, stride=8), :] = two
    out_ref[...] = total_s[...].astype(bf16)


def mix_kernel(*refs):
    parts, refs = refs[:-8], refs[-8:]
    real_ref, imag_ref, out_ref, coef_real_ref, coef_imag_ref, total_s, re_s, im_s = refs
    channels = real_ref.shape[0]
    real, imag = to_lines(parts, total_s, re_s, im_s)
    coef_real_ref[...] = real
    coef_imag_ref[...] = imag
    mixed_real = jnp.zeros(real_ref.shape[1:], f32)
    mixed_imag = jnp.zeros(real_ref.shape[1:], f32)
    for c in range(channels):
        wr, wi = real_ref[c].astype(f32), imag_ref[c].astype(f32)
        re, im = real[c : c + 1], imag[c : c + 1]
        mixed_real = mixed_real + (re * wr - im * wi)
        mixed_imag = mixed_imag + (re * wi + im * wr)
    from_lines(mixed_real, mixed_imag, total_s, re_s, out_ref)


def unmix_kernel(*refs):
    parts, refs = refs[:-10], refs[-10:]
    real_ref, imag_ref, out_ref, mode_real_ref, mode_imag_ref, total_s, re_s, im_s, du_re, du_im = refs
    channels = real_ref.shape[0]
    real, imag = to_lines(parts, total_s, re_s, im_s)
    mode_real_ref[...] = real
    mode_imag_ref[...] = imag
    for c in range(channels):
        wr, wi = real_ref[c].astype(f32), imag_ref[c].astype(f32)
        du_re[c : c + 1, :] = jnp.sum(wr * real + wi * imag, axis=0, keepdims=True)
        du_im[c : c + 1, :] = jnp.sum(wr * imag - wi * real, axis=0, keepdims=True)
    from_lines(du_re[...], du_im[...], total_s, re_s, out_ref)


def owner_stage(kernel, parts, real, imag, extra):
    channels, _, modes = real.shape
    return call(
        kernel,
        (shape(parts[0].shape, bf16), shape((channels, modes), f32), shape((channels, modes), f32)),
        [pltpu.VMEM((4 * channels, 2 * M), f32)]
        + [pltpu.VMEM((2, channels, 2 * M), f32)] * 2
        + [pltpu.VMEM((channels, modes), f32)] * extra,
        8 * real.size,
        parts[0].size * 10 + real.size * 4,
        *parts, real, imag,
    )


def exact(form, left, right):
    return jnp.einsum(form, left, right, precision=lax.Precision.HIGHEST, preferred_element_type=f32)


def at_owner(plan, partial, weight_real, weight_imag, forward, extra=None):
    channels, _, modes = weight_real.shape
    if plan.staged:
        parts = reduce_pieces(plan, partial)
        kernel = mix_kernel if forward else unmix_kernel
        sent, real, imag = owner_stage(kernel, parts, weight_real, weight_imag, 0 if forward else 2)
        pieces, summed = spread_block(plan, sent, extra)
        return pieces, real, imag, summed
    swap = lambda x: lax.all_to_all(x, BOTH, 0, 0, tiled=True)
    pieces = M // modes
    held = (plan.blocks, channels // 2, 4, 2, 2, pieces, modes)
    parts = partial[0].reshape(held).transpose(0, 2, 5, 1, 4, 3, 6)
    parts = swap(parts.reshape(plan.devices, channels, 2, modes))
    total = jnp.sum(parts.astype(f32), axis=0)
    real, imag = total[:, 0], total[:, 1]
    wr, wi = weight_real.astype(f32), weight_imag.astype(f32)
    if forward:
        re = exact("cm,com->om", real, wr) - exact("cm,com->om", imag, wi)
        im = exact("cm,com->om", real, wi) + exact("cm,com->om", imag, wr)
    else:
        re = exact("com,om->cm", wr, real) + exact("com,om->cm", wi, imag)
        im = exact("com,om->cm", wr, imag) - exact("com,om->cm", wi, real)
    sent = jnp.stack([re, im], axis=1).astype(bf16)
    sent = swap(jnp.broadcast_to(sent, (plan.devices,) + sent.shape))
    held = (plan.blocks, 4, pieces, channels // 2, 2, 2, modes)
    spread = sent.reshape(held).transpose(0, 3, 1, 5, 4, 2, 6)
    summed = None if extra is None else lax.psum(extra.astype(f32), BOTH)
    return [spread.reshape(2 * M * channels, 2 * M)], real, imag, summed


def layer(field, cotangent, weight_real, weight_imag, kernel):
    channels, rows_here, cols_here = field.shape
    places_rows, places_cols = lax.axis_size(ROWS), lax.axis_size("cols")
    total_rows, total_cols = rows_here * places_rows, cols_here * places_cols
    scale_rows, scale_cols = 1.0 / math.sqrt(total_rows), 1.0 / math.sqrt(total_cols)
    scale_cells = 1.0 / math.sqrt(total_rows * total_cols)
    all_rows = jnp.asarray(row_table(total_rows, places_rows))
    all_cols = jnp.asarray(col_table(total_cols, places_cols))
    plan = Plan(channels)
    cells = field.size
    modes = 4 * M * M * channels
    transform = 2 * cells * 4 * M + 4 * modes * rows_here
    pieces = plan.shapes(bf16)

    partial = call(
        functools.partial(forward_kernel, plan, scale_rows, scale_cols),
        pieces,
        [
            pltpu.VMEM(field.shape, bf16),
            pltpu.VMEM(all_cols.shape[1:], f32),
            pltpu.VMEM(all_rows.shape[1:], f32),
            pltpu.SemaphoreType.DMA((2 + channels // QUAD,)),
        ],
        transform, cells * 2 + modes * 2,
        field, all_cols, all_rows,
        far=3,
    )
    spectrum, coef_real, coef_imag, _ = at_owner(plan, partial, weight_real, weight_imag, True)
    rows = lax.dynamic_index_in_dim(all_rows, lax.axis_index(ROWS), 0, keepdims=False)
    cols = lax.dynamic_index_in_dim(all_cols, lax.axis_index("cols"), 0, keepdims=False)
    turned, edges = turn(field)
    matrix = band(kernel)
    conv, wide_field = stencil(turned, edges, matrix, channels)

    activated, grad, *partial_grad = call(
        functools.partial(middle_kernel, plan, len(spectrum)),
        (shape(field.shape, bf16), shape(field.shape, bf16)) + pieces,
        [],
        2 * transform, cells * 12 + modes * 4,
        *spectrum, conv, cotangent, rows, cols,
    )
    grad_turned, grad_edges = turn(grad)
    local = kernel_grad_here(wide_field, grad_turned, channels)
    spectrum_grad, mode_real, mode_imag, summed = at_owner(
        plan, partial_grad, weight_real, weight_imag, False, local
    )
    matrix = band(jnp.transpose(kernel[::-1, ::-1], (0, 1, 3, 2)))
    conv_grad, _ = stencil(grad_turned, grad_edges, matrix, channels)
    summed = summed.reshape(summed.shape[0], 128 // channels, channels).transpose(1, 0, 2)
    kernel_grad = summed.reshape(3, 3, channels, channels) * scale_cells

    weight_scale = M * scale_cells
    out_real = (
        coef_real[:, None, :] * mode_real[None] + coef_imag[:, None, :] * mode_imag[None]
    ) * weight_scale
    out_imag = (
        coef_real[:, None, :] * mode_imag[None] - coef_imag[:, None, :] * mode_real[None]
    ) * weight_scale

    field_grad = call(
        functools.partial(last_kernel, plan, len(spectrum_grad), scale_rows, scale_cols),
        shape(field.shape, bf16),
        [],
        transform, cells * 8 + modes * 2,
        *spectrum_grad, conv_grad, rows, cols,
    )
    return activated, field_grad, out_real, out_imag, kernel_grad


def solution(mesh):
    count_rows, count_cols = mesh.shape["rows"], mesh.shape["cols"]
    devices = mesh.devices.reshape(count_rows // 2, 2, count_cols)
    halved = jax.sharding.Mesh(devices, BOTH)
    placed = (
        P(None, ROWS, "cols"),
        P(None, ROWS, "cols"),
        P(None, None, BOTH),
        P(None, None, BOTH),
        P(),
    )
    return jax.shard_map(layer, mesh=halved, in_specs=placed, out_specs=placed, check_vma=False)
```

```python
import functools
import math

import jax
import jax.numpy as jnp
import numpy as np
from jax import lax
from jax.experimental import pallas as pl
from jax.experimental.pallas import tpu as pltpu
from jax.sharding import PartitionSpec as P

M = 64
BLOCK = 8
QUAD = 8
f32 = jnp.float32
bf16 = jnp.bfloat16
ROWS = ("chips", "core")
BOTH = ("chips", "core", "cols")


def dot(left, right):
    return jnp.dot(left, right, preferred_element_type=f32)


def dot_tn(left, right):
    return lax.dot_general(
        left, right, (((0,), (0,)), ((), ())), preferred_element_type=f32
    )


def dot_nt(left, right):
    return lax.dot_general(
        left, right, (((1,), (1,)), ((), ())), preferred_element_type=f32
    )


def call(kernel, out_shape, scratch, flops, moved, *args, far=0):
    near = [pl.BlockSpec(memory_space=pltpu.VMEM)] * (len(args) - far)
    return pl.pallas_call(
        kernel,
        out_shape=out_shape,
        in_specs=[pl.BlockSpec(memory_space=pltpu.HBM)] * far + near,
        out_specs=jax.tree.map(lambda _: pl.BlockSpec(memory_space=pltpu.VMEM), out_shape),
        scratch_shapes=scratch,
        compiler_params=pltpu.CompilerParams(vmem_limit_bytes=20 << 20),
        cost_estimate=pl.CostEstimate(flops=flops, bytes_accessed=moved, transcendentals=0),
    )(*args)


def shape(dims, dtype):
    return jax.ShapeDtypeStruct(dims, dtype)


def row_table(total, places):
    modes = np.concatenate([np.arange(M), total - M + np.arange(M)])
    phase = modes[:, None] * np.arange(total)[None, :] % total
    angle = (phase * (2.0 * np.pi / total)).reshape(2 * M, places, total // places)
    c, s = np.cos(angle).transpose(1, 0, 2), np.sin(angle).transpose(1, 0, 2)
    table = np.stack([np.concatenate([c, s], 2), np.concatenate([-s, c], 2)], axis=2)
    return table.reshape(places, 4 * M, 2 * (total // places)).astype(np.float32)


def col_table(total, places):
    phase = np.arange(total)[:, None] * np.arange(M)[None, :] % total
    angle = (phase * (2.0 * np.pi / total)).reshape(places, total // places, M)
    c, s = np.cos(angle), -np.sin(angle)
    none = np.zeros_like(c)
    even = np.concatenate([c, none, s, none], axis=2)
    odd = np.concatenate([none, c, none, s], axis=2)
    return np.concatenate([even, odd], axis=1).astype(np.float32)


def split(table):
    high = table.astype(bf16)
    return high, (table - high.astype(f32)).astype(bf16)


class Plan:
    def __init__(self, channels):
        self.chips, self.cores, self.cols = (lax.axis_size(a) for a in BOTH)
        self.devices = self.chips * self.cores * self.cols
        self.block = 4 * channels
        self.blocks = M // 2
        self.staged = M == 64 and self.devices == self.blocks

    def shapes(self, dtype):
        if not self.staged:
            return (shape((self.blocks * self.block, 2 * M), dtype),)
        return (shape((self.cols * self.block, 2 * M), dtype),) * (self.cores * self.chips)

    def places(self):
        if not self.staged:
            return [(0, k * self.block) for k in range(self.blocks)]
        return [
            (k, q * self.block) for k in range(self.cores * self.chips) for q in range(self.cols)
        ]

    def rows(self, table_ref):
        if not self.staged:
            return table_ref[...]
        chip, core, col = (lax.axis_index(a) for a in BOTH)
        found = []
        for k in range(self.cores):
            for h in range(self.chips):
                for q in range(self.cols):
                    owner = ((chip ^ h) * self.cores + (core ^ k)) * self.cols + (col ^ q)
                    found.append(table_ref[pl.ds(pl.multiple_of(owner * 8, 8), 8), :])
        return jnp.concatenate(found, axis=0)


def forward_rows(rows):
    return jnp.concatenate(split(rows), axis=1)


def quad_to_modes(plan, cells, cols_table, rows_table, pieces, at):
    height, _ = cells[0].shape
    pairs = [jnp.concatenate(cells[k : k + 2], axis=1) for k in range(0, len(cells), 2)]
    lines = dot(jnp.concatenate(pairs, axis=0), cols_table).astype(bf16)
    for t in range(0, len(pairs), 2):
        sides = []
        for p in (t, t + 1):
            part = lines[p * height : (p + 1) * height]
            sides.append(jnp.concatenate([part[:, : 2 * M], part[:, 2 * M :]], axis=0))
        right = jnp.concatenate(sides, axis=1)
        modes = dot(rows_table, jnp.concatenate([right, right], axis=0))
        for k, (piece, row) in enumerate(plan.places()):
            block = modes[8 * k : 8 * k + 8]
            block = jnp.concatenate([block[:, : 2 * M], block[:, 2 * M :]], axis=0)
            start = row + at + 8 * t
            pieces[piece][start : start + 16, :] = block.astype(bf16)


def quad_to_cells(plan, pieces, at, rows_table, cols_high, cols_low, count):
    stacked = []
    for t in range(0, count // 2, 2):
        first, second = [], []
        for piece, row in plan.places():
            block = pieces[piece][row + at + 8 * t : row + at + 8 * t + 16, :].astype(f32)
            first.append(block[:8])
            second.append(block[8:])
        modes = jnp.concatenate(
            [jnp.concatenate(first, axis=0), jnp.concatenate(second, axis=0)], axis=1
        )
        lines = dot(rows_table, modes.astype(bf16)).astype(bf16)
        height = lines.shape[0] // 2
        for p in (0, 1):
            lanes = slice(2 * M * p, 2 * M * (p + 1))
            stacked.append(jnp.concatenate([lines[:height, lanes], lines[height:, lanes]], axis=1))
    stacked = jnp.concatenate(stacked, axis=0)
    cells = dot_nt(stacked, cols_high) + dot_nt(stacked, cols_low)
    width = cells.shape[1] // 2
    return [
        cells[(k // 2) * height : (k // 2 + 1) * height, (k % 2) * width : (k % 2 + 1) * width]
        for k in range(count)
    ]


def forward_kernel(plan, scale_rows, scale_cols, field_ref, cols_all, rows_all, *refs):
    pieces, (field_s, cols_s, rows_s, sems) = refs[:-4], refs[-4:]
    channels = field_ref.shape[0]
    steps = channels // QUAD
    copies = [
        pltpu.make_async_copy(rows_all.at[lax.axis_index(ROWS)], rows_s, sems.at[0]),
        pltpu.make_async_copy(cols_all.at[lax.axis_index("cols")], cols_s, sems.at[1]),
    ]
    for k in range(steps):
        part = pl.ds(k * QUAD, QUAD)
        copies.append(pltpu.make_async_copy(field_ref.at[part], field_s.at[part], sems.at[2 + k]))
    for copy in copies:
        copy.start()
    copies[0].wait()
    rows_table = forward_rows(plan.rows(rows_s) * scale_rows)
    copies[1].wait()
    cols_table = (cols_s[...] * scale_cols).astype(bf16)
    for k in range(steps):
        copies[2 + k].wait()
        cells = [field_s[k * QUAD + c] for c in range(QUAD)]
        quad_to_modes(plan, cells, cols_table, rows_table, pieces, k * QUAD * 4)


def middle_kernel(plan, count, *refs):
    modes, refs = refs[:count], refs[count:]
    conv_ref, cotangent_ref, rows_ref, cols_ref, out_ref, grad_ref = refs[:6]
    pieces = refs[6:]
    channels = cotangent_ref.shape[0]
    rows = plan.rows(rows_ref)
    rows_in = (rows.T.astype(bf16).astype(f32) / M).astype(bf16)
    rows_out = forward_rows(rows / M)
    cols_high, cols_low = split(cols_ref[...])
    root = math.sqrt(2.0 / math.pi)
    for at in range(0, channels, QUAD):
        cells = quad_to_cells(plan, modes, at * 4, rows_in, cols_high, cols_low, QUAD)
        kept = []
        for k in range(QUAD):
            pre = cells[k] + conv_ref[at + k]
            square = pre * pre
            turn = jnp.tanh(root * (pre + 0.044715 * (square * pre)))
            half = 0.5 * (1.0 + turn)
            out_ref[at + k] = (pre * half).astype(bf16)
            slope = half + 0.5 * pre * (1.0 - turn * turn) * (root * (1.0 + 0.134145 * square))
            grad = (cotangent_ref[at + k].astype(f32) * slope).astype(bf16)
            grad_ref[at + k] = grad
            kept.append(grad)
        quad_to_modes(plan, kept, cols_high, rows_out, pieces, at * 4)


def last_kernel(plan, count, scale_rows, scale_cols, *refs):
    modes = refs[:count]
    conv_ref, rows_ref, cols_ref, out_ref = refs[count:]
    channels = out_ref.shape[0]
    rows_in = (plan.rows(rows_ref) * scale_rows).T.astype(bf16)
    cols_high, cols_low = split(cols_ref[...] * scale_cols)
    for at in range(0, channels, QUAD):
        cells = quad_to_cells(plan, modes, at * 4, rows_in, cols_high, cols_low, QUAD)
        for k in range(QUAD):
            out_ref[at + k] = (cells[k] + conv_ref[at + k]).astype(bf16)


def turn_kernel(cells_ref, turned_ref, edges_ref, turned_s, edges_s):
    channels, height, width = cells_ref.shape
    for c in range(channels):
        turned_s[pl.ds(c, height, stride=channels), :] = cells_ref[c].astype(f32)
    turned = turned_s[...].astype(bf16)
    turned_ref[...] = turned
    row = lax.broadcasted_iota(jnp.int32, (16, width), 0)
    col = lax.broadcasted_iota(jnp.int32, (16, width), 1)
    chosen = ((row == 0) & (col == 0)) | ((row == 1) & (col == width - 1))
    edges = dot_nt(chosen.astype(f32).astype(bf16), turned)
    half = edges_s.shape[0] // 2
    for k in range(half):
        for side in range(2):
            edges_s[side * half + k : side * half + k + 1, :] = edges[
                side : side + 1, k * 128 : (k + 1) * 128
            ]
    edges_ref[...] = edges_s[...].astype(bf16)


def turn(cells):
    channels, height, width = cells.shape
    lines = (height * channels, width)
    return call(
        turn_kernel,
        (shape(lines, bf16), shape((lines[0] // 64, 128), bf16)),
        [pltpu.VMEM(lines, f32), pltpu.VMEM((lines[0] // 64, 128), f32)],
        2 * cells.size * 16, cells.size * 4,
        cells,
    )


def band(weights):
    outs = weights.shape[3]
    flat = jnp.transpose(weights, (3, 0, 1, 2)).reshape(outs, -1)
    step = flat.shape[1] // 3
    rows = [
        jnp.pad(flat, ((0, 0), (step * k, step * (BLOCK - 1 - k)))) for k in range(BLOCK)
    ]
    return jnp.concatenate(rows, axis=0)


def stencil_kernel(turned_ref, left_ref, right_ref, top_ref, low_ref, band_ref, out_ref, wide_ref):
    lines, width = turned_ref.shape
    channels = wide_ref.shape[1] // 3
    row = lax.broadcasted_iota(jnp.int32, (2, width), 0)
    col = lax.broadcasted_iota(jnp.int32, (2, width), 1)
    chosen = ((row == 0) & (col == 0)) | ((row == 1) & (col == width - 1))
    chosen = chosen.astype(f32).astype(bf16)
    where = lax.broadcasted_iota(jnp.int32, (channels, width), 1)

    def widen(at, cells, sides):
        count = cells.shape[0] // channels
        halo = dot_tn(sides, chosen)
        wide = cells.astype(f32)
        before, after = pltpu.roll(wide, 1, 1), pltpu.roll(wide, width - 1, 1)
        for k in range(count):
            part = slice(k * channels, (k + 1) * channels)
            wide_ref[at + k, :channels] = jnp.where(where == 0, halo[part], before[part]).astype(bf16)
            wide_ref[at + k, channels : 2 * channels] = cells[part]
            wide_ref[at + k, 2 * channels :] = jnp.where(
                where == width - 1, halo[part], after[part]
            ).astype(bf16)

    widen(0, top_ref[:channels], top_ref[channels : channels + 2, :channels])
    height = lines // channels
    widen(height + 1, low_ref[:channels], low_ref[channels : channels + 2, :channels])
    step = BLOCK * channels
    left, right = left_ref[...].astype(f32), right_ref[...].astype(f32)
    for b in range(0, lines, step):
        rows = range(b // 128, (b + step) // 128)
        sides = [jnp.concatenate([v[k : k + 1] for k in rows], axis=1) for v in (left, right)]
        sides = jnp.concatenate(sides, axis=0).astype(bf16)
        widen(b // channels + 1, turned_ref[b : b + step], sides)
    matrix = band_ref[...]
    for b in range(0, height // BLOCK, 2):
        pair = [
            wide_ref[BLOCK * k : BLOCK * k + BLOCK + 2].reshape((BLOCK + 2) * 3 * channels, width)
            for k in (b, b + 1)
        ]
        both = dot(matrix, jnp.concatenate(pair, axis=1))
        for k in range(2):
            for i in range(BLOCK):
                line = both[i * channels : (i + 1) * channels, k * width : (k + 1) * width]
                out_ref[pl.ds(BLOCK * (b + k) + i, channels, stride=height), :] = line


def shifted(value, axis, up):
    count = lax.axis_size(axis)
    pairs = [(i, i + 1) if up else (i + 1, i) for i in range(count - 1)]
    return lax.ppermute(value, axis, pairs)


def stencil(turned, edges, sides, matrix, channels):
    lines, width = turned.shape
    height = lines // channels
    if sides is None:
        half = edges.shape[0] // 2
        left = shifted(edges[half:], "cols", True)
        right = shifted(edges[:half], "cols", False)
    else:
        left, right = sides

    def with_sides(cells, at):
        row, lane = at // 128, at % 128
        sides = [v[row : row + 1, lane : lane + channels] for v in (left, right)]
        sides = jnp.concatenate(sides, axis=0)
        return jnp.concatenate([cells, jnp.pad(sides, ((0, 0), (0, width - channels)))], axis=0)

    top = shifted(with_sides(turned[lines - channels :], lines - channels), ROWS, True)
    low = shifted(with_sides(turned[:channels], 0), ROWS, False)
    conv, wide = call(
        stencil_kernel,
        (shape((lines, width), f32), shape((height + 2, 3 * channels, width), bf16)),
        [],
        2 * matrix.size * height * width // BLOCK,
        lines * width * 12 + matrix.size * 2,
        turned, left, right, top, low, matrix,
    )
    return conv.reshape(channels, height, width), wide


def kernel_grad_kernel(cells_ref, grad_ref, out_ref):
    height, lines, width = cells_ref.shape
    taken = grad_ref.shape[0] * BLOCK // (height - 2)
    channels = taken // BLOCK
    total = jnp.zeros(((BLOCK + 2) * lines, taken), f32)
    for b in range(0, (height - 2) // BLOCK, 2):
        cells = [
            cells_ref[BLOCK * k : BLOCK * k + BLOCK + 2].reshape((BLOCK + 2) * lines, width)
            for k in (b, b + 1)
        ]
        grads = [grad_ref[taken * k : taken * (k + 1)] for k in (b, b + 1)]
        total = total + dot_nt(jnp.concatenate(cells, axis=1), jnp.concatenate(grads, axis=1))
    place = lax.broadcasted_iota(jnp.int32, (3 * lines, taken), 1) // channels
    folded = jnp.zeros((3 * lines, taken), f32)
    for k in range(BLOCK):
        folded = folded + jnp.where(place == k, total[lines * k : lines * (k + 3)], 0.0)
    size = taken
    while size > 128:
        size //= 2
        folded = folded[:, :size] + folded[:, size : 2 * size]
    step = size // 2
    while step >= channels:
        folded = folded + pltpu.roll(folded, step, 1)
        step //= 2
    groups = size // channels
    rows = 3 * lines // groups
    place = lax.broadcasted_iota(jnp.int32, (rows, size), 1) // channels
    packed = jnp.zeros((rows, size), f32)
    for k in range(groups):
        packed = packed + jnp.where(place == k, folded[rows * k : rows * (k + 1)], 0.0)
    out_ref[...] = packed.astype(bf16)


def kernel_grad_here(cells, grad, channels):
    _, lines, _ = cells.shape
    return call(
        kernel_grad_kernel,
        shape((3 * lines * channels // 128, 128), bf16),
        [],
        2 * cells.size * BLOCK * channels,
        cells.size * 2 + grad.size * 2,
        cells, grad,
    )


def swapped(value, axis, step):
    count = lax.axis_size(axis)
    return lax.ppermute(value, axis, [(i, i ^ step) for i in range(count)])


def tree_sum(values):
    values = [v.astype(f32) for v in values]
    while len(values) > 1:
        values = [values[k] + values[k + 1] for k in range(0, len(values), 2)]
    return values[0]


def reduce_pieces(plan, pieces):
    kept, sent = pieces[: plan.chips], pieces[plan.chips :]
    chips = []
    for h in reversed(range(plan.chips)):
        total = kept[h].astype(f32) + swapped(sent[h], "core", 1).astype(f32)
        chips.append(swapped(total.astype(bf16), "chips", h) if h else total)
    total = tree_sum(chips)
    parts = []
    for q in reversed(range(plan.cols)):
        part = total[q * plan.block : (q + 1) * plan.block].astype(bf16)
        parts.append(swapped(part, "cols", q) if q else part)
    return parts


def spread_block(plan, block, edges, extra=None):
    def widen(parts, axis, count):
        whole = parts[0] if len(parts) == 1 else jnp.concatenate(parts, axis=0)
        got = {q: swapped(whole, axis, q) for q in reversed(range(1, count))}
        got[0] = whole
        found, at = [], 0
        for part in parts:
            found.append([got[q][at : at + part.shape[0]] for q in range(count)])
            at += part.shape[0]
        return found

    more = [] if extra is None else [extra]
    blocks, around, *more = widen([block, edges] + more, "cols", plan.cols)
    more = [tree_sum(v).astype(bf16) for v in more]
    col, half = lax.axis_index("cols"), edges.shape[0] // 2
    left = right = jnp.zeros((half, edges.shape[1]), bf16)
    for q in range(1, plan.cols):
        left = jnp.where((col ^ q) == col - 1, around[q][half:], left)
        right = jnp.where((col ^ q) == col + 1, around[q][:half], right)
    pieces, *more = widen([jnp.concatenate(blocks, axis=0)] + more, "chips", plan.chips)
    more = [tree_sum(v).astype(bf16) for v in more]
    more = [tree_sum([v, swapped(v, "core", 1)]) for v in more]
    pieces = pieces + [swapped(v, "core", 1) for v in pieces]
    return pieces, (left, right), more[0] if more else None


def to_lines(parts, total_s, re_s, im_s):
    total = parts[0][...].astype(f32)
    for part in parts[1:]:
        total = total + part[...].astype(f32)
    total_s[...] = total
    pairs = total.shape[0] // 8
    low = lax.broadcasted_iota(jnp.int32, (pairs, 2 * M), 1) < M
    for side, held in enumerate((re_s, im_s)):
        for t in range(2):
            one = total_s[pl.ds(4 * t + side, pairs, stride=8), :]
            two = total_s[pl.ds(4 * t + 2 + side, pairs, stride=8), :]
            even = jnp.where(low, one, pltpu.roll(two, M, 1))
            odd = jnp.where(low, pltpu.roll(one, M, 1), two)
            held[t, pl.ds(0, pairs, stride=2), :] = even
            held[t, pl.ds(1, pairs, stride=2), :] = odd
    return tuple(jnp.concatenate([held[0], held[1]], axis=1) for held in (re_s, im_s))


def from_lines(real, imag, total_s, re_s, out_ref):
    pairs = real.shape[0] // 2
    low = lax.broadcasted_iota(jnp.int32, (pairs, 2 * M), 1) < M
    for side, value in enumerate((real, imag)):
        for t in range(2):
            re_s[t] = value[:, 2 * M * t : 2 * M * (t + 1)]
            even = re_s[t, pl.ds(0, pairs, stride=2), :]
            odd = re_s[t, pl.ds(1, pairs, stride=2), :]
            one = jnp.where(low, even, pltpu.roll(odd, M, 1))
            two = jnp.where(low, pltpu.roll(even, M, 1), odd)
            total_s[pl.ds(4 * t + side, pairs, stride=8), :] = one
            total_s[pl.ds(4 * t + 2 + side, pairs, stride=8), :] = two
    out_ref[...] = total_s[...].astype(bf16)


def mix_kernel(*refs):
    parts, refs = refs[:-8], refs[-8:]
    real_ref, imag_ref, out_ref, coef_real_ref, coef_imag_ref, total_s, re_s, im_s = refs
    channels = real_ref.shape[0]
    real, imag = to_lines(parts, total_s, re_s, im_s)
    coef_real_ref[...] = real
    coef_imag_ref[...] = imag
    mixed_real = jnp.zeros(real_ref.shape[1:], f32)
    mixed_imag = jnp.zeros(real_ref.shape[1:], f32)
    for c in range(channels):
        wr, wi = real_ref[c].astype(f32), imag_ref[c].astype(f32)
        re, im = real[c : c + 1], imag[c : c + 1]
        mixed_real = mixed_real + (re * wr - im * wi)
        mixed_imag = mixed_imag + (re * wi + im * wr)
    from_lines(mixed_real, mixed_imag, total_s, re_s, out_ref)


def unmix_kernel(*refs):
    parts, refs = refs[:-10], refs[-10:]
    real_ref, imag_ref, out_ref, mode_real_ref, mode_imag_ref, total_s, re_s, im_s, du_re, du_im = refs
    channels = real_ref.shape[0]
    real, imag = to_lines(parts, total_s, re_s, im_s)
    mode_real_ref[...] = real
    mode_imag_ref[...] = imag
    for c in range(channels):
        wr, wi = real_ref[c].astype(f32), imag_ref[c].astype(f32)
        du_re[c : c + 1, :] = jnp.sum(wr * real + wi * imag, axis=0, keepdims=True)
        du_im[c : c + 1, :] = jnp.sum(wr * imag - wi * real, axis=0, keepdims=True)
    from_lines(du_re[...], du_im[...], total_s, re_s, out_ref)


def owner_stage(kernel, parts, real, imag, extra):
    channels, _, modes = real.shape
    return call(
        kernel,
        (shape(parts[0].shape, bf16), shape((channels, modes), f32), shape((channels, modes), f32)),
        [pltpu.VMEM((4 * channels, 2 * M), f32)]
        + [pltpu.VMEM((2, channels, 2 * M), f32)] * 2
        + [pltpu.VMEM((channels, modes), f32)] * extra,
        8 * real.size,
        parts[0].size * 10 + real.size * 4,
        *parts, real, imag,
    )


def exact(form, left, right):
    return jnp.einsum(form, left, right, precision=lax.Precision.HIGHEST, preferred_element_type=f32)


def at_owner(plan, partial, weight_real, weight_imag, forward, edges, extra=None):
    channels, _, modes = weight_real.shape
    if plan.staged:
        parts = reduce_pieces(plan, partial)
        kernel = mix_kernel if forward else unmix_kernel
        sent, real, imag = owner_stage(kernel, parts, weight_real, weight_imag, 0 if forward else 2)
        pieces, sides, summed = spread_block(plan, sent, edges, extra)
        return pieces, real, imag, sides, summed
    swap = lambda x: lax.all_to_all(x, BOTH, 0, 0, tiled=True)
    pieces = M // modes
    held = (plan.blocks, channels // 2, 4, 2, 2, pieces, modes)
    parts = partial[0].reshape(held).transpose(0, 2, 5, 1, 4, 3, 6)
    parts = swap(parts.reshape(plan.devices, channels, 2, modes))
    total = jnp.sum(parts.astype(f32), axis=0)
    real, imag = total[:, 0], total[:, 1]
    wr, wi = weight_real.astype(f32), weight_imag.astype(f32)
    if forward:
        re = exact("cm,com->om", real, wr) - exact("cm,com->om", imag, wi)
        im = exact("cm,com->om", real, wi) + exact("cm,com->om", imag, wr)
    else:
        re = exact("com,om->cm", wr, real) + exact("com,om->cm", wi, imag)
        im = exact("com,om->cm", wr, imag) - exact("com,om->cm", wi, real)
    sent = jnp.stack([re, im], axis=1).astype(bf16)
    sent = swap(jnp.broadcast_to(sent, (plan.devices,) + sent.shape))
    held = (plan.blocks, 4, pieces, channels // 2, 2, 2, modes)
    spread = sent.reshape(held).transpose(0, 3, 1, 5, 4, 2, 6)
    summed = None if extra is None else lax.psum(extra.astype(f32), BOTH)
    return [spread.reshape(2 * M * channels, 2 * M)], real, imag, None, summed


def layer(field, cotangent, weight_real, weight_imag, kernel):
    channels, rows_here, cols_here = field.shape
    places_rows, places_cols = lax.axis_size(ROWS), lax.axis_size("cols")
    total_rows, total_cols = rows_here * places_rows, cols_here * places_cols
    scale_rows, scale_cols = 1.0 / math.sqrt(total_rows), 1.0 / math.sqrt(total_cols)
    scale_cells = 1.0 / math.sqrt(total_rows * total_cols)
    all_rows = jnp.asarray(row_table(total_rows, places_rows))
    all_cols = jnp.asarray(col_table(total_cols, places_cols))
    plan = Plan(channels)
    cells = field.size
    modes = 4 * M * M * channels
    transform = 2 * cells * 4 * M + 4 * modes * rows_here
    pieces = plan.shapes(bf16)

    partial = call(
        functools.partial(forward_kernel, plan, scale_rows, scale_cols),
        pieces,
        [
            pltpu.VMEM(field.shape, bf16),
            pltpu.VMEM(all_cols.shape[1:], f32),
            pltpu.VMEM(all_rows.shape[1:], f32),
            pltpu.SemaphoreType.DMA((2 + channels // QUAD,)),
        ],
        transform, cells * 2 + modes * 2,
        *(pltpu.with_memory_space_constraint(v, pltpu.HBM) for v in (field, all_cols, all_rows)),
        far=3,
    )
    rows = lax.dynamic_index_in_dim(all_rows, lax.axis_index(ROWS), 0, keepdims=False)
    cols = lax.dynamic_index_in_dim(all_cols, lax.axis_index("cols"), 0, keepdims=False)
    turned, edges = turn(field)
    spectrum, coef_real, coef_imag, sides, _ = at_owner(
        plan, partial, weight_real, weight_imag, True, edges
    )
    matrix = band(kernel)
    conv, wide_field = stencil(turned, edges, sides, matrix, channels)

    activated, grad, *partial_grad = call(
        functools.partial(middle_kernel, plan, len(spectrum)),
        (shape(field.shape, bf16), shape(field.shape, bf16)) + pieces,
        [],
        2 * transform, cells * 12 + modes * 4,
        *spectrum, conv, cotangent, rows, cols,
    )
    grad_turned, grad_edges = turn(grad)
    local = kernel_grad_here(wide_field, grad_turned, channels)
    spectrum_grad, mode_real, mode_imag, sides, summed = at_owner(
        plan, partial_grad, weight_real, weight_imag, False, grad_edges, local
    )
    matrix = band(jnp.transpose(kernel[::-1, ::-1], (0, 1, 3, 2)))
    conv_grad, _ = stencil(grad_turned, grad_edges, sides, matrix, channels)
    summed = summed.reshape(summed.shape[0], 128 // channels, channels).transpose(1, 0, 2)
    kernel_grad = summed.reshape(3, 3, channels, channels) * scale_cells

    weight_scale = M * scale_cells
    out_real = (
        coef_real[:, None, :] * mode_real[None] + coef_imag[:, None, :] * mode_imag[None]
    ) * weight_scale
    out_imag = (
        coef_real[:, None, :] * mode_imag[None] - coef_imag[:, None, :] * mode_real[None]
    ) * weight_scale

    field_grad = call(
        functools.partial(last_kernel, plan, len(spectrum_grad), scale_rows, scale_cols),
        shape(field.shape, bf16),
        [],
        transform, cells * 8 + modes * 2,
        *spectrum_grad, conv_grad, rows, cols,
    )
    return activated, field_grad, out_real, out_imag, kernel_grad


def solution(mesh):
    count_rows, count_cols = mesh.shape["rows"], mesh.shape["cols"]
    devices = mesh.devices.reshape(count_rows // 2, 2, count_cols)
    halved = jax.sharding.Mesh(devices, BOTH)
    placed = (
        P(None, ROWS, "cols"),
        P(None, ROWS, "cols"),
        P(None, None, BOTH),
        P(None, None, BOTH),
        P(),
    )
    return jax.shard_map(layer, mesh=halved, in_specs=placed, out_specs=placed, check_vma=False)
```

```python
import functools
import math

import jax
import jax.numpy as jnp
import numpy as np
from jax import lax
from jax.experimental import pallas as pl
from jax.experimental.pallas import tpu as pltpu
from jax.sharding import PartitionSpec as P

M = 64
BLOCK = 8
PART = 8
f32 = jnp.float32
bf16 = jnp.bfloat16
ROWS = ("chips", "core")
BOTH = ("chips", "core", "cols")


def dot(left, right):
    return jnp.dot(left, right, preferred_element_type=f32)


def dot_tn(left, right):
    return lax.dot_general(
        left, right, (((0,), (0,)), ((), ())), preferred_element_type=f32
    )


def dot_nt(left, right):
    return lax.dot_general(
        left, right, (((1,), (1,)), ((), ())), preferred_element_type=f32
    )


def call(kernel, out_shape, scratch, flops, moved, *args, far=0, far_out=0):
    many = len(jax.tree.leaves(out_shape))
    spaces = [pltpu.HBM] * far_out + [pltpu.VMEM] * (many - far_out)
    out_specs = [pl.BlockSpec(memory_space=m) for m in spaces]
    near = [pl.BlockSpec(memory_space=pltpu.VMEM)] * (len(args) - far)
    return pl.pallas_call(
        kernel,
        out_shape=out_shape,
        in_specs=[pl.BlockSpec(memory_space=pltpu.HBM)] * far + near,
        out_specs=jax.tree.unflatten(jax.tree.structure(out_shape), out_specs),
        scratch_shapes=scratch,
        compiler_params=pltpu.CompilerParams(vmem_limit_bytes=20 << 20),
        cost_estimate=pl.CostEstimate(flops=flops, bytes_accessed=moved, transcendentals=0),
    )(*args)


def shape(dims, dtype):
    return jax.ShapeDtypeStruct(dims, dtype)


def row_table(total, places):
    modes = np.concatenate([np.arange(M), total - M + np.arange(M)])
    phase = modes[:, None] * np.arange(total)[None, :] % total
    angle = (phase * (2.0 * np.pi / total)).reshape(2 * M, places, total // places)
    c, s = np.cos(angle).transpose(1, 0, 2), np.sin(angle).transpose(1, 0, 2)
    table = np.stack([np.concatenate([c, s], 2), np.concatenate([-s, c], 2)], axis=2)
    return table.reshape(places, 4 * M, 2 * (total // places)).astype(np.float32)


def col_table(total, places):
    phase = np.arange(total)[:, None] * np.arange(M)[None, :] % total
    angle = (phase * (2.0 * np.pi / total)).reshape(places, total // places, M)
    c, s = np.cos(angle), -np.sin(angle)
    none = np.zeros_like(c)
    even = np.concatenate([c, none, s, none], axis=2)
    odd = np.concatenate([none, c, none, s], axis=2)
    return np.concatenate([even, odd], axis=1).astype(np.float32)


def split(table):
    high = table.astype(bf16)
    return high, (table - high.astype(f32)).astype(bf16)


class Plan:
    def __init__(self, channels):
        self.chips, self.cores, self.cols = (lax.axis_size(a) for a in BOTH)
        self.devices = self.chips * self.cores * self.cols
        self.block = 4 * channels
        self.blocks = M // 2
        self.staged = M == 64 and self.devices == self.blocks

    def shapes(self, dtype):
        if not self.staged:
            return (shape((self.blocks * self.block, 2 * M), dtype),)
        return (shape((self.cols * self.block, 2 * M), dtype),) * (self.cores * self.chips)

    def places(self):
        if not self.staged:
            return [(0, k * self.block) for k in range(self.blocks)]
        return [
            (k, q * self.block) for k in range(self.cores * self.chips) for q in range(self.cols)
        ]

    def rows(self, table_ref):
        if not self.staged:
            return table_ref[...]
        chip, core, col = (lax.axis_index(a) for a in BOTH)
        found = []
        for k in range(self.cores):
            for h in range(self.chips):
                for q in range(self.cols):
                    owner = ((chip ^ h) * self.cores + (core ^ k)) * self.cols + (col ^ q)
                    found.append(table_ref[pl.ds(pl.multiple_of(owner * 8, 8), 8), :])
        return jnp.concatenate(found, axis=0)


def forward_rows(rows):
    return jnp.concatenate(split(rows), axis=1)


def to_modes(plan, cells, cols_table, rows_table, pieces):
    height, _ = cells[0].shape
    pairs = [jnp.concatenate(cells[k : k + 2], axis=1) for k in range(0, len(cells), 2)]
    lines = dot(jnp.concatenate(pairs, axis=0), cols_table).astype(bf16)
    for t in range(0, len(pairs), 2):
        sides = []
        for p in (t, t + 1):
            part = lines[p * height : (p + 1) * height]
            sides.append(jnp.concatenate([part[:, : 2 * M], part[:, 2 * M :]], axis=0))
        right = jnp.concatenate(sides, axis=1)
        modes = dot(rows_table, jnp.concatenate([right, right], axis=0))
        for k, (piece, row) in enumerate(plan.places()):
            block = modes[8 * k : 8 * k + 8]
            block = jnp.concatenate([block[:, : 2 * M], block[:, 2 * M :]], axis=0)
            start = row + 8 * t
            pieces[piece][start : start + 16, :] = block.astype(bf16)


def to_cells(plan, pieces, rows_table, cols_table, count):
    stacked = []
    for t in range(0, count // 2, 2):
        first, second = [], []
        for piece, row in plan.places():
            block = pieces[piece][row + 8 * t : row + 8 * t + 16, :].astype(f32)
            first.append(block[:8])
            second.append(block[8:])
        modes = jnp.concatenate(
            [jnp.concatenate(first, axis=0), jnp.concatenate(second, axis=0)], axis=1
        )
        lines = dot(rows_table, modes.astype(bf16)).astype(bf16)
        height = lines.shape[0] // 2
        for p in (0, 1):
            lanes = slice(2 * M * p, 2 * M * (p + 1))
            halves = [lines[:height, lanes], lines[height:, lanes]]
            stacked.append(jnp.concatenate(halves + halves, axis=1))
    cells = dot_nt(jnp.concatenate(stacked, axis=0), cols_table)
    width = cells.shape[1] // 2
    return [
        cells[(k // 2) * height : (k // 2 + 1) * height, (k % 2) * width : (k % 2 + 1) * width]
        for k in range(count)
    ]


def forward_kernel(plan, scale_rows, scale_cols, field_ref, cols_all, rows_all, *refs):
    pieces, (field_s, cols_s, rows_s, sems) = refs[:-4], refs[-4:]
    channels = field_ref.shape[0]
    copies = [
        pltpu.make_async_copy(rows_all.at[lax.axis_index(ROWS)], rows_s, sems.at[0]),
        pltpu.make_async_copy(cols_all.at[lax.axis_index("cols")], cols_s, sems.at[1]),
    ]
    for k in range(channels // PART):
        part = pl.ds(k * PART, PART)
        copies.append(pltpu.make_async_copy(field_ref.at[part], field_s.at[part], sems.at[2 + k]))
    for copy in copies:
        copy.start()
    copies[0].wait()
    rows_table = forward_rows(plan.rows(rows_s) * scale_rows)
    copies[1].wait()
    cols_table = (cols_s[...] * scale_cols).astype(bf16)
    for copy in copies[2:]:
        copy.wait()
    to_modes(plan, [field_s[c] for c in range(channels)], cols_table, rows_table, pieces)


def middle_kernel(plan, count, *refs):
    modes, refs = refs[:count], refs[count:]
    conv_ref, cotangent_ref, rows_ref, cols_ref, out_hbm, grad_ref = refs[:6]
    pieces, (out_s, sem) = refs[6:-2], refs[-2:]
    channels = cotangent_ref.shape[0]
    rows = plan.rows(rows_ref)
    rows_in = (rows.T.astype(bf16).astype(f32) / M).astype(bf16)
    rows_out = forward_rows(rows / M)
    cols_pair = split(cols_ref[...])
    root = math.sqrt(2.0 / math.pi)
    cells = to_cells(plan, modes, rows_in, jnp.concatenate(cols_pair, axis=1), channels)
    kept = []
    for c in range(channels):
        pre = cells[c] + conv_ref[c]
        square = pre * pre
        turn = jnp.tanh(pre * (root + (root * 0.044715) * square))
        half = 0.5 + 0.5 * turn
        out = pre * half
        out_s[c] = out.astype(bf16)
        slope = half + (out * (1.0 - half)) * (2.0 * root + (6.0 * root * 0.044715) * square)
        grad = (cotangent_ref[c].astype(f32) * slope).astype(bf16)
        grad_ref[c] = grad
        kept.append(grad)
    copy = pltpu.make_async_copy(out_s, out_hbm, sem)
    copy.start()
    to_modes(plan, kept, cols_pair[0], rows_out, pieces)
    copy.wait()


def last_kernel(plan, count, scale_rows, scale_cols, *refs):
    modes = refs[:count]
    conv_ref, rows_ref, cols_ref, sums_ref, out_ref, kernel_ref = refs[count:]
    channels = out_ref.shape[0]
    rows_in = (plan.rows(rows_ref) * scale_rows).T.astype(bf16)
    cols_pair = split(cols_ref[...] * scale_cols)
    cells = to_cells(plan, modes, rows_in, jnp.concatenate(cols_pair, axis=1), channels)
    for c in range(channels):
        out_ref[c] = (cells[c] + conv_ref[c]).astype(bf16)
    sums = sums_ref[...] * (scale_rows * scale_cols)
    rows, width = sums.shape
    for g in range(width // channels):
        group = (sums if g == 0 else pltpu.roll(sums, width - g * channels, 1))[:, :channels]
        for k in range(0, rows, 8):
            line = g * rows + k
            at = line % channels
            kernel_ref[line // channels, at : at + 8, :] = group[k : k + 8]


def turn_kernel(cells_ref, turned_ref, edges_ref, turned_s, edges_s):
    channels, height, width = cells_ref.shape
    for c in range(channels):
        turned_s[pl.ds(c, height, stride=channels), :] = cells_ref[c].astype(f32)
    turned = turned_s[...].astype(bf16)
    turned_ref[...] = turned
    row = lax.broadcasted_iota(jnp.int32, (16, width), 0)
    col = lax.broadcasted_iota(jnp.int32, (16, width), 1)
    chosen = ((row == 0) & (col == 0)) | ((row == 1) & (col == width - 1))
    edges = dot_nt(chosen.astype(f32).astype(bf16), turned)
    half = edges_s.shape[0] // 2
    for k in range(half):
        for side in range(2):
            edges_s[side * half + k : side * half + k + 1, :] = edges[
                side : side + 1, k * 128 : (k + 1) * 128
            ]
    edges_ref[...] = edges_s[...].astype(bf16)


def turn(cells):
    channels, height, width = cells.shape
    lines = (height * channels, width)
    return call(
        turn_kernel,
        (shape(lines, bf16), shape((lines[0] // 64, 128), bf16)),
        [pltpu.VMEM(lines, f32), pltpu.VMEM((lines[0] // 64, 128), f32)],
        2 * cells.size * 16, cells.size * 4,
        cells,
    )


def corner_kernel(edges_ref, top_ref, low_ref, out_ref):
    rows, width = edges_ref.shape
    row = lax.broadcasted_iota(jnp.int32, (16, width), 0)
    col = lax.broadcasted_iota(jnp.int32, (16, width), 1)
    chosen = ((row == 0) & (col == 0)) | ((row == 1) & (col == width - 1))
    ends = jnp.concatenate([top_ref[...], low_ref[...]], axis=0)
    cells = dot_nt(chosen.astype(f32).astype(bf16), ends)
    none = jnp.zeros((16, width - cells.shape[1]), f32)
    out_ref[:rows] = edges_ref[...]
    out_ref[rows:] = jnp.concatenate([cells, none], axis=1).astype(bf16)


def with_corners(edges, top, low):
    rows, width = edges.shape
    return call(
        corner_kernel, shape((rows + 16, width), bf16), [], 0, edges.size * 6, edges, top, low
    )


def band(weights):
    outs = weights.shape[3]
    flat = jnp.transpose(weights, (3, 0, 1, 2)).reshape(outs, -1)
    step = flat.shape[1] // 3
    rows = [
        jnp.pad(flat, ((0, 0), (step * k, step * (BLOCK - 1 - k)))) for k in range(BLOCK)
    ]
    return jnp.concatenate(rows, axis=0)


def stencil_kernel(turned_ref, left_ref, right_ref, top_ref, low_ref, band_ref, out_ref, wide_ref):
    lines, width = turned_ref.shape
    channels = wide_ref.shape[1] // 3
    row = lax.broadcasted_iota(jnp.int32, (2, width), 0)
    col = lax.broadcasted_iota(jnp.int32, (2, width), 1)
    chosen = ((row == 0) & (col == 0)) | ((row == 1) & (col == width - 1))
    chosen = chosen.astype(f32).astype(bf16)
    where = lax.broadcasted_iota(jnp.int32, (channels, width), 1)

    def widen(at, cells, sides):
        count = cells.shape[0] // channels
        halo = dot_tn(sides, chosen)
        wide = cells.astype(f32)
        before, after = pltpu.roll(wide, 1, 1), pltpu.roll(wide, width - 1, 1)
        for k in range(count):
            part = slice(k * channels, (k + 1) * channels)
            wide_ref[at + k, :channels] = jnp.where(where == 0, halo[part], before[part]).astype(bf16)
            wide_ref[at + k, channels : 2 * channels] = cells[part]
            wide_ref[at + k, 2 * channels :] = jnp.where(
                where == width - 1, halo[part], after[part]
            ).astype(bf16)

    height = lines // channels
    step = BLOCK * channels
    left, right = left_ref[...].astype(f32), right_ref[...].astype(f32)
    half = (left.shape[0] - 16) // 2
    corners = jnp.concatenate([left[2 * half + 1 :][:1], right[2 * half :][:1]], axis=0)
    corners = corners.astype(bf16)
    widen(0, top_ref[...], corners[:, :channels])
    widen(height + 1, low_ref[...], corners[:, channels : 2 * channels])
    left, right = left[half : 2 * half], right[:half]
    for b in range(0, lines, step):
        rows = range(b // 128, (b + step) // 128)
        sides = [jnp.concatenate([v[k : k + 1] for k in rows], axis=1) for v in (left, right)]
        sides = jnp.concatenate(sides, axis=0).astype(bf16)
        widen(b // channels + 1, turned_ref[b : b + step], sides)
    matrix = band_ref[...]
    for b in range(0, height // BLOCK, 2):
        pair = [
            wide_ref[BLOCK * k : BLOCK * k + BLOCK + 2].reshape((BLOCK + 2) * 3 * channels, width)
            for k in (b, b + 1)
        ]
        both = dot(matrix, jnp.concatenate(pair, axis=1))
        for k in range(2):
            for i in range(BLOCK):
                line = both[i * channels : (i + 1) * channels, k * width : (k + 1) * width]
                out_ref[pl.ds(BLOCK * (b + k) + i, channels, stride=height), :] = line


def shifted(value, axis, up):
    count = lax.axis_size(axis)
    pairs = [(i, i + 1) if up else (i + 1, i) for i in range(count - 1)]
    return lax.ppermute(value, axis, pairs)


def ends_of(turned, channels):
    top = shifted(turned[turned.shape[0] - channels :], ROWS, True)
    low = shifted(turned[:channels], ROWS, False)
    return top, low


def stencil(turned, ends, edges, sides, matrix, channels):
    lines, width = turned.shape
    height = lines // channels
    if sides is None:
        left = shifted(edges, "cols", True)
        right = shifted(edges, "cols", False)
    else:
        left, right = sides
    top, low = ends
    conv, wide = call(
        stencil_kernel,
        (shape((lines, width), f32), shape((height + 2, 3 * channels, width), bf16)),
        [],
        2 * matrix.size * height * width // BLOCK,
        lines * width * 12 + matrix.size * 2,
        turned, left, right, top, low, matrix,
    )
    return conv.reshape(channels, height, width), wide


def kernel_grad_kernel(cells_ref, grad_ref, out_ref):
    height, lines, width = cells_ref.shape
    taken = grad_ref.shape[0] * BLOCK // (height - 2)
    channels = taken // BLOCK
    total = jnp.zeros(((BLOCK + 2) * lines, taken), f32)
    for b in range(0, (height - 2) // BLOCK, 2):
        cells = [
            cells_ref[BLOCK * k : BLOCK * k + BLOCK + 2].reshape((BLOCK + 2) * lines, width)
            for k in (b, b + 1)
        ]
        grads = [grad_ref[taken * k : taken * (k + 1)] for k in (b, b + 1)]
        total = total + dot_nt(jnp.concatenate(cells, axis=1), jnp.concatenate(grads, axis=1))
    place = lax.broadcasted_iota(jnp.int32, (3 * lines, taken), 1) // channels
    folded = jnp.zeros((3 * lines, taken), f32)
    for k in range(BLOCK):
        folded = folded + jnp.where(place == k, total[lines * k : lines * (k + 3)], 0.0)
    size = taken
    while size > 128:
        size //= 2
        folded = folded[:, :size] + folded[:, size : 2 * size]
    step = size // 2
    while step >= channels:
        folded = folded + pltpu.roll(folded, step, 1)
        step //= 2
    groups = size // channels
    rows = 3 * lines // groups
    place = lax.broadcasted_iota(jnp.int32, (rows, size), 1) // channels
    packed = jnp.zeros((rows, size), f32)
    for k in range(groups):
        packed = packed + jnp.where(place == k, folded[rows * k : rows * (k + 1)], 0.0)
    out_ref[...] = packed.astype(bf16)


def kernel_grad_here(cells, grad, channels):
    _, lines, _ = cells.shape
    return call(
        kernel_grad_kernel,
        shape((3 * lines * channels // 128, 128), bf16),
        [],
        2 * cells.size * BLOCK * channels,
        cells.size * 2 + grad.size * 2,
        cells, grad,
    )


def swapped(value, axis, step):
    count = lax.axis_size(axis)
    return lax.ppermute(value, axis, [(i, i ^ step) for i in range(count)])


def tree_sum(values):
    values = [v.astype(f32) for v in values]
    while len(values) > 1:
        values = [values[k] + values[k + 1] for k in range(0, len(values), 2)]
    return values[0]


def reduce_pieces(plan, pieces):
    kept, sent = pieces[: plan.chips], pieces[plan.chips :]
    chips = []
    for h in reversed(range(plan.chips)):
        total = kept[h].astype(f32) + swapped(sent[h], "core", 1).astype(f32)
        chips.append(swapped(total.astype(bf16), "chips", h) if h else total)
    total = tree_sum(chips)
    parts = []
    for q in reversed(range(plan.cols)):
        part = total[q * plan.block : (q + 1) * plan.block].astype(bf16)
        parts.append(swapped(part, "cols", q) if q else part)
    return parts


def spread_block(plan, block, edges, extra=None):
    def widen(parts, axis, count):
        whole = parts[0] if len(parts) == 1 else jnp.concatenate(parts, axis=0)
        got = {q: swapped(whole, axis, q) for q in reversed(range(1, count))}
        got[0] = whole
        found, at = [], 0
        for part in parts:
            found.append([got[q][at : at + part.shape[0]] for q in range(count)])
            at += part.shape[0]
        return found

    more = [] if extra is None else [extra]
    blocks, around, *more = widen([block, edges] + more, "cols", plan.cols)
    more = [tree_sum(v).astype(bf16) for v in more]
    col = lax.axis_index("cols")
    left = right = jnp.zeros(edges.shape, bf16)
    for q in range(1, plan.cols):
        left = jnp.where((col ^ q) == col - 1, around[q], left)
        right = jnp.where((col ^ q) == col + 1, around[q], right)
    pieces, *more = widen([jnp.concatenate(blocks, axis=0)] + more, "chips", plan.chips)
    more = [tree_sum(v).astype(bf16) for v in more]
    more = [tree_sum([v, swapped(v, "core", 1)]) for v in more]
    pieces = pieces + [swapped(v, "core", 1) for v in pieces]
    return pieces, (left, right), more[0] if more else None


def to_lines(parts, total_s, re_s, im_s):
    total = parts[0][...].astype(f32)
    for part in parts[1:]:
        total = total + part[...].astype(f32)
    total_s[...] = total
    pairs = total.shape[0] // 8
    low = lax.broadcasted_iota(jnp.int32, (pairs, 2 * M), 1) < M
    for side, held in enumerate((re_s, im_s)):
        for t in range(2):
            one = total_s[pl.ds(4 * t + side, pairs, stride=8), :]
            two = total_s[pl.ds(4 * t + 2 + side, pairs, stride=8), :]
            even = jnp.where(low, one, pltpu.roll(two, M, 1))
            odd = jnp.where(low, pltpu.roll(one, M, 1), two)
            held[t, pl.ds(0, pairs, stride=2), :] = even
            held[t, pl.ds(1, pairs, stride=2), :] = odd
    return tuple(jnp.concatenate([held[0], held[1]], axis=1) for held in (re_s, im_s))


def from_lines(real, imag, total_s, re_s, out_ref):
    pairs = real.shape[0] // 2
    low = lax.broadcasted_iota(jnp.int32, (pairs, 2 * M), 1) < M
    for side, value in enumerate((real, imag)):
        for t in range(2):
            re_s[t] = value[:, 2 * M * t : 2 * M * (t + 1)]
            even = re_s[t, pl.ds(0, pairs, stride=2), :]
            odd = re_s[t, pl.ds(1, pairs, stride=2), :]
            one = jnp.where(low, even, pltpu.roll(odd, M, 1))
            two = jnp.where(low, pltpu.roll(even, M, 1), odd)
            total_s[pl.ds(4 * t + side, pairs, stride=8), :] = one
            total_s[pl.ds(4 * t + 2 + side, pairs, stride=8), :] = two
    out_ref[...] = total_s[...].astype(bf16)


def mix_kernel(*refs):
    parts, refs = refs[:-8], refs[-8:]
    real_ref, imag_ref, out_ref, coef_real_ref, coef_imag_ref, total_s, re_s, im_s = refs
    channels = real_ref.shape[0]
    real, imag = to_lines(parts, total_s, re_s, im_s)
    coef_real_ref[...] = real
    coef_imag_ref[...] = imag
    mixed_real = jnp.zeros(real_ref.shape[1:], f32)
    mixed_imag = jnp.zeros(real_ref.shape[1:], f32)
    for c in range(channels):
        wr, wi = real_ref[c].astype(f32), imag_ref[c].astype(f32)
        re, im = real[c : c + 1], imag[c : c + 1]
        mixed_real = mixed_real + (re * wr - im * wi)
        mixed_imag = mixed_imag + (re * wi + im * wr)
    from_lines(mixed_real, mixed_imag, total_s, re_s, out_ref)


def unmix_kernel(*refs):
    parts, refs = refs[:-10], refs[-10:]
    real_ref, imag_ref, out_ref, mode_real_ref, mode_imag_ref, total_s, re_s, im_s, du_re, du_im = refs
    channels = real_ref.shape[0]
    real, imag = to_lines(parts, total_s, re_s, im_s)
    mode_real_ref[...] = real
    mode_imag_ref[...] = imag
    for c in range(channels):
        wr, wi = real_ref[c].astype(f32), imag_ref[c].astype(f32)
        du_re[c : c + 1, :] = jnp.sum(wr * real + wi * imag, axis=0, keepdims=True)
        du_im[c : c + 1, :] = jnp.sum(wr * imag - wi * real, axis=0, keepdims=True)
    from_lines(du_re[...], du_im[...], total_s, re_s, out_ref)


def owner_stage(kernel, parts, real, imag, extra):
    channels, _, modes = real.shape
    return call(
        kernel,
        (shape(parts[0].shape, bf16), shape((channels, modes), f32), shape((channels, modes), f32)),
        [pltpu.VMEM((4 * channels, 2 * M), f32)]
        + [pltpu.VMEM((2, channels, 2 * M), f32)] * 2
        + [pltpu.VMEM((channels, modes), f32)] * extra,
        8 * real.size,
        parts[0].size * 10 + real.size * 4,
        *parts, real, imag,
    )


def exact(form, left, right):
    return jnp.einsum(form, left, right, precision=lax.Precision.HIGHEST, preferred_element_type=f32)


def at_owner(plan, partial, weight_real, weight_imag, forward, edges, extra=None):
    channels, _, modes = weight_real.shape
    if plan.staged:
        parts = reduce_pieces(plan, partial)
        kernel = mix_kernel if forward else unmix_kernel
        sent, real, imag = owner_stage(kernel, parts, weight_real, weight_imag, 0 if forward else 2)
        pieces, sides, summed = spread_block(plan, sent, edges, extra)
        return pieces, real, imag, sides, summed
    swap = lambda x: lax.all_to_all(x, BOTH, 0, 0, tiled=True)
    pieces = M // modes
    held = (plan.blocks, channels // 2, 4, 2, 2, pieces, modes)
    parts = partial[0].reshape(held).transpose(0, 2, 5, 1, 4, 3, 6)
    parts = swap(parts.reshape(plan.devices, channels, 2, modes))
    total = jnp.sum(parts.astype(f32), axis=0)
    real, imag = total[:, 0], total[:, 1]
    wr, wi = weight_real.astype(f32), weight_imag.astype(f32)
    if forward:
        re = exact("cm,com->om", real, wr) - exact("cm,com->om", imag, wi)
        im = exact("cm,com->om", real, wi) + exact("cm,com->om", imag, wr)
    else:
        re = exact("com,om->cm", wr, real) + exact("com,om->cm", wi, imag)
        im = exact("com,om->cm", wr, imag) - exact("com,om->cm", wi, real)
    sent = jnp.stack([re, im], axis=1).astype(bf16)
    sent = swap(jnp.broadcast_to(sent, (plan.devices,) + sent.shape))
    held = (plan.blocks, 4, pieces, channels // 2, 2, 2, modes)
    spread = sent.reshape(held).transpose(0, 3, 1, 5, 4, 2, 6)
    summed = None if extra is None else lax.psum(extra.astype(f32), BOTH)
    return [spread.reshape(2 * M * channels, 2 * M)], real, imag, None, summed


def layer(field, cotangent, weight_real, weight_imag, kernel):
    channels, rows_here, cols_here = field.shape
    places_rows, places_cols = lax.axis_size(ROWS), lax.axis_size("cols")
    total_rows, total_cols = rows_here * places_rows, cols_here * places_cols
    scale_rows, scale_cols = 1.0 / math.sqrt(total_rows), 1.0 / math.sqrt(total_cols)
    scale_cells = 1.0 / math.sqrt(total_rows * total_cols)
    all_rows = jnp.asarray(row_table(total_rows, places_rows))
    all_cols = jnp.asarray(col_table(total_cols, places_cols))
    plan = Plan(channels)
    cells = field.size
    modes = 4 * M * M * channels
    transform = 2 * cells * 4 * M + 4 * modes * rows_here
    pieces = plan.shapes(bf16)

    partial = call(
        functools.partial(forward_kernel, plan, scale_rows, scale_cols),
        pieces,
        [
            pltpu.VMEM(field.shape, bf16),
            pltpu.VMEM(all_cols.shape[1:], f32),
            pltpu.VMEM(all_rows.shape[1:], f32),
            pltpu.SemaphoreType.DMA((2 + channels // PART,)),
        ],
        transform, cells * 2 + modes * 2,
        *(pltpu.with_memory_space_constraint(v, pltpu.HBM) for v in (field, all_cols, all_rows)),
        far=3,
    )
    rows = lax.dynamic_index_in_dim(all_rows, lax.axis_index(ROWS), 0, keepdims=False)
    cols = lax.dynamic_index_in_dim(all_cols, lax.axis_index("cols"), 0, keepdims=False)
    turned, edges = turn(field)
    ends = ends_of(turned, channels)
    edges = with_corners(edges, *ends)
    spectrum, coef_real, coef_imag, sides, _ = at_owner(
        plan, partial, weight_real, weight_imag, True, edges
    )
    matrix = band(kernel)
    conv, wide_field = stencil(turned, ends, edges, sides, matrix, channels)

    activated, grad, *partial_grad = call(
        functools.partial(middle_kernel, plan, len(spectrum)),
        (shape(field.shape, bf16), shape(field.shape, bf16)) + pieces,
        [pltpu.VMEM(field.shape, bf16), pltpu.SemaphoreType.DMA],
        2 * transform, cells * 12 + modes * 4,
        *spectrum, conv, cotangent, rows, cols,
        far_out=1,
    )
    grad_turned, grad_edges = turn(grad)
    grad_ends = ends_of(grad_turned, channels)
    grad_edges = with_corners(grad_edges, *grad_ends)
    local = kernel_grad_here(wide_field, grad_turned, channels)
    spectrum_grad, mode_real, mode_imag, sides, summed = at_owner(
        plan, partial_grad, weight_real, weight_imag, False, grad_edges, local
    )
    matrix = band(jnp.transpose(kernel[::-1, ::-1], (0, 1, 3, 2)))
    conv_grad, _ = stencil(grad_turned, grad_ends, grad_edges, sides, matrix, channels)
    weight_scale = M * scale_cells
    out_real = (
        coef_real[:, None, :] * mode_real[None] + coef_imag[:, None, :] * mode_imag[None]
    ) * weight_scale
    out_imag = (
        coef_real[:, None, :] * mode_imag[None] - coef_imag[:, None, :] * mode_real[None]
    ) * weight_scale

    field_grad, kernel_grad = call(
        functools.partial(last_kernel, plan, len(spectrum_grad), scale_rows, scale_cols),
        (shape(field.shape, bf16), shape((9, channels, channels), f32)),
        [],
        transform, cells * 8 + modes * 2,
        *spectrum_grad, conv_grad, rows, cols, summed,
    )
    kernel_grad = kernel_grad.reshape(kernel.shape)
    return activated, field_grad, out_real, out_imag, kernel_grad


def solution(mesh):
    count_rows, count_cols = mesh.shape["rows"], mesh.shape["cols"]
    devices = mesh.devices.reshape(count_rows // 2, 2, count_cols)
    halved = jax.sharding.Mesh(devices, BOTH)
    placed = (
        P(None, ROWS, "cols"),
        P(None, ROWS, "cols"),
        P(None, None, BOTH),
        P(None, None, BOTH),
        P(),
    )
    return jax.shard_map(layer, mesh=halved, in_specs=placed, out_specs=placed, check_vma=False)
```
